32 devices in a mesh: group: 4 (over x, core), member: 8 (over z, y).
Axes of the slice: x: 2, y: 2, z: 4, core: 2. Of those that a mesh axis runs over, the one named last changes fastest.
Arguments:
- right_side: float32 [32, 256, 4096], P(None, 'group', 'member'), may hold values from -8 to 8
- diagonal: float32 [256, 4096], P('group', 'member'), may hold values from 0.02 to 1
- face_weight: float32 [2, 256, 4096], P(None, 'group', 'member'), may hold values from 0.5 to 2
- aggregation: int32 [256, 4096], P('group', 'member'), may hold values from 0 to 127, as said below
Outputs:
- solution_field: float32 [32, 256, 4096], P(None, 'group', 'member')
The draws below stay inside these ranges and needn't reach their ends.
Inputs may be any that keep to these rules, and one draw needn't show every extreme that they name: `aggregation`: each cell names one aggregate of its own device block; the aggregates are irregular patches.
All inputs are finite; a program needn't handle non-finite values.
Results may differ from the reference program's by a relative error of at most 0.0003.
Values sent between devices are 32-bit elements; how exact they have to be, the bound alone decides.
A program may use at most 128 MiB of HBM per device.

```python
import math
import jax
import jax.numpy as jnp
from jax import lax

R = 32
CX = 64
CY = 512
AGG = 128
PRE = 2
POST = 2
CHEB = 6
NX = 256
NY = 4096
N_GROUP = 4
N_MEMBER = 8


def draw_aggregation(key, part):
    xs = lax.broadcasted_iota(jnp.int32, (NX, NY), 0)
    ys = lax.broadcasted_iota(jnp.int32, (NX, NY), 1)
    local_x = xs % CX
    local_y = ys % CY
    key_x, key_y = jax.random.split(jax.random.fold_in(key, 17))
    off_x = jax.random.randint(key_x, (NX, NY), -1, 2)
    off_y = jax.random.randint(key_y, (NX, NY), -2, 3)
    near_x = jnp.clip(local_x + off_x, 0, CX - 1)
    near_y = jnp.clip(local_y + off_y, 0, CY - 1)
    splits = min(CX, max(1, AGG * 4 // CY))
    height = max(1, CY * splits // AGG)
    tile = near_y // height * splits + near_x * splits // CX
    block = xs // CX * 3 + ys // CY * 7
    return ((tile * 37 + block * 11) % AGG).astype(jnp.int32)


def shard_levels(key, extent, cuts, smallest, high):
    gain, own = 1.0, jax.random.fold_in(key, 6)
    for axis_at, blocks in cuts:
        draws = jnp.exp(jax.random.uniform(jax.random.fold_in(own, axis_at), (blocks,), jnp.float32, smallest / len(cuts), high / len(cuts)))
        gain = gain * jnp.repeat(draws, extent[axis_at] // blocks).reshape([-1 if axis == axis_at else 1 for axis in range(len(extent))])
    return gain


def scatter_about(own_key, dims, deviation, limit, cuts=(), kind=jnp.bfloat16):
    entries = jax.random.normal(own_key, dims, jnp.float32) * deviation
    if len(cuts) > 0:
        entries = shard_levels(own_key, dims, cuts, -0.22, 0.18) * entries
    return jnp.clip(entries, min=-limit, max=limit).astype(kind)


def setup_inputs(seed: int = 0) -> dict:
    streams_of = jax.random.split(jax.random.key(seed), 5)
    right_side = scatter_about(streams_of[0], (R, NX, NY), 1.0, 8.0, ((1, 4), (2, 8)), jnp.float32)
    diagonal = jnp.clip(jnp.exp(math.log(1.0) - 3.912023 * jax.random.uniform(streams_of[1], (NX, NY), jnp.float32) ** shard_levels(streams_of[1], (NX, NY), ((0, 4), (1, 8)), -0.2, 0.2)), 0.02, 1.0)
    face_weight = jnp.clip(jnp.exp(math.log(2.0) - 1.3862944 * jax.random.uniform(streams_of[2], (2, NX, NY), jnp.float32) ** shard_levels(streams_of[2], (2, NX, NY), ((1, 4), (2, 8)), -0.2, 0.2)), 0.5, 2.0)
    aggregation = draw_aggregation(jax.random.fold_in(streams_of[4], 71), 0)
    return dict(right_side=right_side, diagonal=diagonal, face_weight=face_weight, aggregation=aggregation)


OMEGA = 0.8
RATIO = 30.0
HIGH_LEVEL = lax.Precision.HIGHEST


def lower_faces(wx, wy):
    wx_low = jnp.pad(wx, ((1, 0), (0, 0)))[:-1, :]
    wy_low = jnp.pad(wy, ((0, 0), (1, 0)))[:, :-1]
    return wx_low, wy_low


def stencil(field, diagf, wx, wy):
    wx_low, wy_low = lower_faces(wx, wy)
    padded = jnp.pad(field, ((0, 0), (1, 1), (1, 1)))
    beside = wx * padded[:, 2:, 1:-1] + wx_low * padded[:, :-2, 1:-1]
    beside = beside + wy * padded[:, 1:-1, 2:] + wy_low * padded[:, 1:-1, :-2]
    return diagf * field - beside


def smooth(field, rhs, diagf, wx, wy):
    return field + OMEGA * (rhs - stencil(field, diagf, wx, wy)) / diagf


def chebyshev(rhs, matvec, lmax):
    lmin = lmax / RATIO
    theta = (lmax + lmin) / 2.0
    delta = (lmax - lmin) / 2.0
    sigma = theta / delta
    rho = 1.0 / sigma
    sol = jnp.zeros_like(rhs)
    resid = rhs
    direc = rhs / theta
    for step in range(CHEB):
        sol = sol + direc
        if step + 1 < CHEB:
            resid = resid - matvec(direc)
            rho_new = 1.0 / (2.0 * sigma - rho)
            direc = rho_new * rho * direc + (2.0 * rho_new / delta) * resid
            rho = rho_new
    return sol


def coarse_product(input_vector, block_diagonal, block_lower):
    zero_vec = jnp.zeros_like(input_vector[:1])
    prior_columns = jnp.concatenate([zero_vec, input_vector[:-1]], axis=0)
    upper_band = jnp.einsum("fwg,fge->fwe", input_vector, block_lower, precision=HIGH_LEVEL)
    next_weight = jnp.concatenate([upper_band[1:], zero_vec], axis=0)
    return jnp.einsum("ioc,iqc->ioq", input_vector, block_diagonal, precision=HIGH_LEVEL) + jnp.einsum("ioc,iqc->ioq", prior_columns, block_lower, precision=HIGH_LEVEL) + next_weight


def bound_of(block_diagonal, block_lower):
    row_d = jnp.sum(jnp.abs(block_diagonal), axis=2)
    row_l = jnp.sum(jnp.abs(block_lower), axis=2)
    col_l = jnp.sum(jnp.abs(block_lower), axis=1)
    col_next = jnp.concatenate([col_l[1:], jnp.zeros_like(col_l[:1])], axis=0)
    return jnp.max(row_d + row_l + col_next)


def group_correction(args):
    agg_g, diag_g, wx_g, wy_g, resid_g = args
    labels = jnp.arange(AGG, dtype=jnp.int32)

    def per_block(block_args):
        agg_b, diag_b, wx_b, wy_b, resid_b = block_args
        onehot = (agg_b[None, :, :] == labels[:, None, None]).astype(jnp.float32)
        applied = stencil(onehot, diag_b, wx_b, wy_b)
        block_diagonal = jnp.einsum("axy,bxy->ab", onehot, applied, precision=HIGH_LEVEL)
        rhs_b = jnp.einsum("rxy,axy->ra", resid_b, onehot, precision=HIGH_LEVEL)
        return block_diagonal, rhs_b

    block_diagonal, coarse_rhs = lax.map(per_block, (agg_g, diag_g, wx_g, wy_g, resid_g))
    tops = agg_g[:, :, -1] + 1
    prevs = jnp.concatenate([jnp.zeros_like(tops[:1]), tops[:-1]], axis=0)
    last_weight = wy_g[:, :, -1]
    prev_weight = jnp.concatenate([jnp.zeros_like(last_weight[:1]), last_weight[:-1]], axis=0)
    prev_hot = (prevs[:, :, None] == (labels + 1)[None, None, :]).astype(jnp.float32)
    bottom_hot = (agg_g[:, :, 0][:, :, None] == labels[None, None, :]).astype(jnp.float32)
    block_lower = -jnp.einsum("mxa,mxb->mab", bottom_hot * prev_weight[:, :, None], prev_hot, precision=HIGH_LEVEL)
    lmax = bound_of(block_diagonal, block_lower)
    sol = chebyshev(coarse_rhs, lambda v: coarse_product(v, block_diagonal, block_lower), lmax)

    def expand(block_args):
        agg_b, sol_b = block_args
        onehot = (agg_b[None, :, :] == labels[:, None, None]).astype(jnp.float32)
        return jnp.einsum("ra,axy->rxy", sol_b, onehot, precision=HIGH_LEVEL)

    return lax.map(expand, (agg_g, sol))


def reference(right_side, diagonal, face_weight, aggregation):
    wx = face_weight[0]
    wy = face_weight[1]
    wx_low, wy_low = lower_faces(wx, wy)
    diagf = diagonal + wx + wy + wx_low + wy_low
    field = OMEGA * right_side / diagf
    for step in range(PRE - 1):
        field = smooth(field, right_side, diagf, wx, wy)
    resid = right_side - stencil(field, diagf, wx, wy)
    agg4 = aggregation.reshape(N_GROUP, CX, N_MEMBER, CY).transpose(0, 2, 1, 3)
    diag4 = diagf.reshape(N_GROUP, CX, N_MEMBER, CY).transpose(0, 2, 1, 3)
    wx4 = wx.reshape(N_GROUP, CX, N_MEMBER, CY).transpose(0, 2, 1, 3)
    wy4 = wy.reshape(N_GROUP, CX, N_MEMBER, CY).transpose(0, 2, 1, 3)
    resid5 = resid.reshape(R, N_GROUP, CX, N_MEMBER, CY).transpose(1, 3, 0, 2, 4)
    corr = lax.map(group_correction, (agg4, diag4, wx4, wy4, resid5))
    corr = corr.transpose(2, 0, 3, 1, 4).reshape(R, NX, NY)
    field = field + corr
    for step in range(POST):
        field = smooth(field, right_side, diagf, wx, wy)
    return field
```

```python
import functools

import jax
import jax.numpy as jnp
from jax import lax
from jax.experimental import pallas as pl
from jax.experimental.pallas import tpu as pltpu
from jax.sharding import PartitionSpec as P

AGG = 128
POST = 2
CHEB = 6
OMEGA = 0.8
RATIO = 30.0
LANES = 128
MESH = pl.DeviceIdType.MESH
F32 = jnp.float32
BF16 = jnp.bfloat16
NT = (((1,), (1,)), ((), ()))


def split(value):
    high = value.astype(BF16)
    return high, (value - high.astype(F32)).astype(BF16)


AX, AX_LOW, AY, AY_LOW, Q, Q_INV = range(6)
LABEL, LABEL_X, LABEL_Y, X_HIGH, X_LOW, Y_HIGH, Y_LOW, G_HIGH, G_LOW = range(6, 15)
PLANES = 15
D_BLOCK = 16
NEAR = (-2, -1, 1, 2)
FAR = (-3, -2, -1, 1, 2, 3)


def cycle_kernel(
    n_group, n_member, rhs_hbm, diag_ref, face_ref, agg_ref, out_ref,
    rhs, cf, hot, acc, low_row_ref, below_w_ref, below_a_ref, above_a_ref,
    b, f, g, h, col_send, col_recv, dir_send, dir_recv, lm_send, lm_recv,
    w_send, w_recv, state_send, state_recv,
    rhs_sem, w_ssem, w_rsem, state_ssem, state_rsem, edge_ssem, edge_rsem, halo_ssem, halo_rsem, dir_ssem, dir_rsem, lm_ssem, lm_rsem,
):
    rows, n_rhs, width = rhs.shape
    tiles = width // LANES
    gi = lax.axis_index("group")
    mi = lax.axis_index("member")
    g_up, g_down = lax.rem(gi + 1, n_group), lax.rem(gi + n_group - 1, n_group)
    m_up, m_down = lax.rem(mi + 1, n_member), lax.rem(mi + n_member - 1, n_member)

    def member_at(off):
        return lax.rem(mi + off + n_member, n_member)

    def fetch(x):
        return pltpu.make_async_copy(rhs_hbm.at[:, x, :], rhs.at[x], rhs_sem.at[x])

    def start_fetch(x, carry):
        fetch(x).start()
        return carry

    lax.fori_loop(0, rows, start_fetch, 0)

    barrier = pltpu.get_barrier_semaphore()
    for peer in (g_up, g_down):
        pl.semaphore_signal(barrier, inc=1, device_id=(peer, mi), device_id_type=MESH)
    for off in range(1, n_member):
        peer = lax.rem(mi + off, n_member)
        pl.semaphore_signal(barrier, inc=1, device_id=(gi, peer), device_id_type=MESH)

    lane = lax.broadcasted_iota(jnp.int32, (n_rhs, LANES), 1)
    label = lax.broadcasted_iota(jnp.int32, (AGG, width), 0).astype(F32).astype(BF16)
    one, none = jnp.ones((), BF16), jnp.zeros((), BF16)

    def remote(src, dst, ssem, rsem, target):
        return pltpu.make_async_remote_copy(
            src_ref=src, dst_ref=dst, send_sem=ssem, recv_sem=rsem,
            device_id=target, device_id_type=MESH,
        )

    def exchange(phase, buf):
        plan = (
            (buf.at[rows], buf.at[0], (g_up, mi)),
            (buf.at[1], buf.at[rows + 1], (g_down, mi)),
            (col_send.at[phase, 0], col_recv.at[phase, 0], (gi, m_up)),
            (col_send.at[phase, 1], col_recv.at[phase, 1], (gi, m_down)),
        )
        copies = [
            remote(s, d, halo_ssem.at[phase, i], halo_rsem.at[phase, i], t)
            for i, (s, d, t) in enumerate(plan)
        ]
        for copy in copies:
            copy.start()
        return copies

    started = []

    def finish(copies):
        for copy in copies:
            copy.wait_recv()
        started.extend(copies)

    def pack(x, value, carry):
        last, first = carry
        last = jnp.where(lane == x + 1, pltpu.roll(value[:, value.shape[1] - LANES:], x + 2, 1), last)
        first = jnp.where(lane == x, pltpu.roll(value[:, :LANES], x, 1), first)
        return last, first

    def store_columns(phase, carry):
        col_send[phase, 0] = carry[0]
        col_send[phase, 1] = carry[1]

    empty = (jnp.zeros((n_rhs, LANES), F32), jnp.zeros((n_rhs, LANES), F32))

    def neighbours(buf, x):
        cur = buf[x + 1]
        parts = [cur[:, k * LANES:(k + 1) * LANES] for k in range(tiles)]
        zero = jnp.zeros((n_rhs, LANES), F32)
        right = [zero] + [pltpu.roll(p, 1, 1) for p in parts]
        left = [pltpu.roll(p, LANES - 1, 1) for p in parts] + [zero]
        low = [jnp.where(lane == 0, right[k], right[k + 1]) for k in range(tiles)]
        high = [jnp.where(lane == LANES - 1, left[k + 1], left[k]) for k in range(tiles)]
        low = jnp.concatenate(low, axis=1)
        high = jnp.concatenate(high, axis=1)
        total = cf[AX, pl.ds(x, 1), :] * buf[x + 2] + cf[AX_LOW, pl.ds(x, 1), :] * buf[x]
        return cur, total + cf[AY, pl.ds(x, 1), :] * high + cf[AY_LOW, pl.ds(x, 1), :] * low

    def patch(phase, x):
        before = pltpu.roll(col_recv[phase, 0], 127 - x, 1)
        after = pltpu.roll(col_recv[phase, 1], 127 - x, 1)
        low = jnp.where(lane == 0, before, 0.0) * cf[AY_LOW, pl.ds(x, 1), :][:, :LANES]
        high = jnp.where(lane == LANES - 1, after, 0.0) * cf[AY, pl.ds(x, 1), :][:, width - LANES:]
        return low, high

    def sweep(phase, copies, body, dest, shift, unroll):
        def inner(x, carry):
            dest[x + shift] = body(x)
            return carry

        lax.fori_loop(1, rows - 1, inner, 0, unroll=unroll)
        finish(copies)
        inner(0, 0)
        inner(rows - 1, 0)

        def outer(x, carry):
            low, high = patch(phase, x)
            first = dest[x + shift, :, :LANES] + low
            last = dest[x + shift, :, width - LANES:] + high
            dest[x + shift, :, :LANES] = first
            dest[x + shift, :, width - LANES:] = last
            return pack(x, jnp.concatenate([first, last], axis=1), carry)

        return lax.fori_loop(0, rows, outer, empty, unroll=16)

    def row(plane, x):
        return cf[plane, pl.ds(x, 1), :]

    def narrow(plane, x):
        return jnp.broadcast_to(row(plane, x), (16, width)).astype(BF16)

    def spread_row(plane, x):
        return jnp.concatenate([narrow(plane, x)] * (AGG // 16), axis=0)

    wx, wy, agg = face_ref[0], face_ref[1], agg_ref[...].astype(F32)
    xs = lax.broadcasted_iota(jnp.int32, (rows, width), 0)
    ys = lax.broadcasted_iota(jnp.int32, (rows, width), 1)
    wx_low = jnp.where(xs == 0, 0.0, pltpu.roll(wx, 1, 0))
    wy_low = jnp.where(ys == 0, 0.0, pltpu.roll(wy, 1, 1))
    own_diag = diag_ref[...] + wx + wy + wx_low + wy_low
    cf[LABEL] = agg
    cf[LABEL_X] = pltpu.roll(agg, rows - 1, 0)
    cf[LABEL_Y] = pltpu.roll(agg, width - 1, 1)
    inner_y = jnp.where(ys == width - 1, 0.0, wy)
    inner_x = jnp.where(xs == rows - 1, 0.0, wx)
    inner_x = inner_x + jnp.where(cf[LABEL_X] == cf[LABEL_Y], inner_y, 0.0)
    for plane, value in ((X_HIGH, inner_x), (Y_HIGH, inner_y), (G_HIGH, own_diag)):
        high = value.astype(BF16).astype(F32)
        cf[plane] = high
        cf[plane + 1] = value - high
    acc[...] = jnp.zeros_like(acc)

    pl.semaphore_wait(barrier, n_member + 1)
    edges = [
        remote(s, d, edge_ssem.at[i], edge_rsem.at[i], t)
        for i, (s, d, t) in enumerate((
            (face_ref.at[0, pl.ds(rows - 8, 8), :], low_row_ref, (g_up, mi)),
            (face_ref.at[1, :, pl.ds(width - LANES, LANES)], below_w_ref, (gi, m_up)),
            (agg_ref.at[:, pl.ds(width - LANES, LANES)], below_a_ref, (gi, m_up)),
            (agg_ref.at[:, pl.ds(0, LANES)], above_a_ref, (gi, m_down)),
        ))
    ]
    for copy in edges:
        copy.start()

    side = lax.broadcasted_iota(jnp.int32, (16, width), 0) < 8

    def pairs(block, carry):
        def one_row(i, total):
            x = block * D_BLOCK + i
            own = jnp.where(label == spread_row(LABEL, x), one, none)
            hot[x] = own
            at_x = label == spread_row(LABEL_X, x)
            at_y = label == spread_row(LABEL_Y, x)
            high = jnp.where(at_y, spread_row(Y_HIGH, x), none)
            high = jnp.where(at_x, spread_row(X_HIGH, x), high)
            low = jnp.where(at_y, spread_row(Y_LOW, x), none)
            low = jnp.where(at_x, spread_row(X_LOW, x), low)
            gain = jnp.where(side, row(G_HIGH, x), row(G_LOW, x)).astype(BF16)
            both = jnp.concatenate([high, low, gain], axis=0)
            return total + lax.dot_general(both, own, NT, preferred_element_type=F32)

        acc[...] += lax.fori_loop(
            0, D_BLOCK, one_row, jnp.zeros(acc.shape, F32), unroll=D_BLOCK
        )
        return carry

    blocks = rows // D_BLOCK
    early = blocks // 2
    lax.fori_loop(0, early, pairs, 0)
    finish(edges)

    low_row = jnp.where(gi > 0, low_row_ref[7:8, :], 0.0)
    below = jnp.where(mi > 0, below_w_ref[:, LANES - 1:], 0.0)
    wx_low = wx_low + jnp.where(xs == 0, low_row, 0.0)
    wy_low = wy_low + jnp.where(ys == 0, below, 0.0)
    diagf = diag_ref[...] + wx + wy + wx_low + wy_low
    q = OMEGA / diagf
    last_x = (xs == rows - 1) & (gi == n_group - 1)
    last_y = (ys == width - 1) & (mi == n_member - 1)
    cf[AX] = jnp.where(last_x, 0.0, q * wx)
    cf[AX_LOW] = q * wx_low
    cf[AY] = jnp.where(last_y, 0.0, q * wy)
    cf[AY_LOW] = q * wy_low
    cf[Q] = q
    cf[Q_INV] = diagf * (1.0 / OMEGA)

    def scale(x, carry):
        fetch(x).wait()
        value = rhs[x] * row(Q, x)
        b[x + 1] = value
        return pack(x, value, carry)

    store_columns(0, lax.fori_loop(0, rows, scale, empty, unroll=8))
    first = exchange(0, b)
    lax.fori_loop(early, blocks, pairs, 0)

    def dot_high(left, right):
        return jnp.dot(
            left, right, precision=lax.Precision.HIGHEST, preferred_element_type=F32
        )

    lab = lax.broadcasted_iota(jnp.int32, (rows, LANES), 1)

    def hot_column(column):
        return jnp.where(column == lab, 1.0, 0.0)

    first_hot = hot_column(agg_ref[:, 0:1])
    last_hot = hot_column(agg_ref[:, width - 1:])
    below_hot = hot_column(below_a_ref[:, LANES - 1:])
    above_hot = hot_column(above_a_ref[:, 0:1])
    above = jnp.where(mi < n_member - 1, face_ref[1, :, width - 1:], 0.0)
    half = dot_high(first_hot.T, first_hot * (0.5 * below))
    half = half - acc[:AGG] - acc[AGG:2 * AGG]
    low_sum = jnp.sum(hot[0].astype(F32) * low_row, axis=1, keepdims=True)
    eye = lax.broadcasted_iota(jnp.int32, (AGG, AGG), 0)
    eye = eye == lax.broadcasted_iota(jnp.int32, (AGG, AGG), 1)
    gain = acc[2 * AGG:2 * AGG + 1] + acc[2 * AGG + 8:2 * AGG + 9]
    half = half + jnp.where(eye, 0.5 * (low_sum + gain), 0.0)
    w = jnp.concatenate(
        [
            half + half.T,
            -dot_high(below_hot.T, first_hot * below),
            -dot_high(above_hot.T, last_hot * above),
        ],
        axis=0,
    )
    lm = jnp.sum(jnp.abs(w), axis=0, keepdims=True)
    lm_send[...] = jnp.broadcast_to(lm, lm_send.shape)
    lm_copies = []
    for off in range(1, n_member):
        peer = lax.rem(mi + off, n_member)
        copy = remote(
            lm_send, lm_recv.at[off - 1], lm_ssem.at[off - 1], lm_rsem.at[off - 1], (gi, peer)
        )
        copy.start()
        lm_copies.append(copy)
    w_send[...] = w
    w_copies = {}
    for i, off in enumerate(NEAR):
        w_copies[-off] = (i, remote(
            w_send, w_recv.at[i], w_ssem.at[i], w_rsem.at[i], (gi, member_at(off))
        ))
        w_copies[-off][1].start()

    def pre(x):
        cur, total = neighbours(b, x)
        return (2.0 - OMEGA) * cur + total

    store_columns(1, sweep(0, first, pre, f, 1, 8))
    second = exchange(1, f)

    def restrict(x, carry):
        cur, total = neighbours(f, x)
        resid = (b[x + 1] - OMEGA * cur + total) * row(Q_INV, x)
        high, low = split(resid)
        both = jnp.concatenate([high, low], axis=0)
        return carry + lax.dot_general(both, hot[x], NT, preferred_element_type=F32)

    sums = lax.fori_loop(
        1, rows - 1, restrict, jnp.zeros((2 * n_rhs, AGG), F32), unroll=16
    )
    finish(second)
    sums = restrict(rows - 1, restrict(0, sums))
    resid = sums[:n_rhs] + sums[n_rhs:]
    resid = resid + dot_high(
        pltpu.roll(col_recv[1, 0], LANES - 1, 1)[:, :rows], first_hot * below
    )
    resid = resid + dot_high(col_recv[1, 1][:, :rows], last_hot * above)

    finish(lm_copies)
    lm8 = lm_send[...]
    for off in range(1, n_member):
        lm8 = jnp.maximum(lm8, lm_recv[off - 1])
    lmax = jnp.max(lm8[0:1], axis=1, keepdims=True)
    lmin = lmax / RATIO
    theta = (lmax + lmin) / 2.0
    delta = (lmax - lmin) / 2.0
    sigma = theta / delta
    rho = 1.0 / sigma
    finish([copy for _, copy in w_copies.values()])
    blocks_w = {0: split(w_send[...])}
    for off, (i, _) in w_copies.items():
        blocks_w[off] = split(w_recv[i])

    def product(at, dirs):
        w_high, w_low = blocks_w[at]
        vec = jnp.concatenate([dirs[at], dirs[at - 1], dirs[at + 1]], axis=1)
        v_high, v_low = split(vec)
        both = jnp.concatenate([v_high, v_low], axis=0)
        prod = jnp.dot(both, w_high, preferred_element_type=F32)
        prod = prod[:n_rhs] + prod[n_rhs:]
        return prod + jnp.dot(v_high, w_low, preferred_element_type=F32)

    def gather(send, recv, ssem, rsem, offsets):
        copies = [
            remote(send, recv.at[i], ssem.at[i], rsem.at[i], (gi, member_at(off)))
            for i, off in enumerate(offsets)
        ]
        for copy in copies:
            copy.start()
        finish(copies)

    dirs = {0: resid / theta}
    dir_send[...] = dirs[0]
    gather(dir_send, dir_recv, dir_ssem, dir_rsem, FAR)
    res = {0: resid}
    for i, off in enumerate(FAR):
        dirs[-off] = dir_recv[i]
        res[-off] = dirs[-off] * theta
    reach = 3
    sol = jnp.zeros_like(resid)
    for step in range(CHEB):
        sol = sol + dirs[0]
        if step + 1 < CHEB:
            if reach == 0:
                state_send[0] = dirs[0]
                state_send[1] = res[0]
                gather(state_send, state_recv, state_ssem, state_rsem, NEAR)
                for i, off in enumerate(NEAR):
                    dirs[-off] = state_recv[i, 0]
                    res[-off] = state_recv[i, 1]
                reach = 2
            reach -= 1
            rho_new = 1.0 / (2.0 * sigma - rho)
            own_scale, res_scale = rho_new * rho, 2.0 * rho_new / delta
            inside = range(-reach, reach + 1)
            res = {at: res[at] - product(at, dirs) for at in inside}
            dirs = {at: own_scale * dirs[at] + res_scale * res[at] for at in inside}
            rho = rho_new

    e_high, e_low = split(sol)
    e_both = jnp.concatenate([e_high, e_low], axis=0)

    def prolong(x, carry):
        spread = jnp.dot(e_both, hot[x], preferred_element_type=F32)
        value = f[x + 1] + spread[:n_rhs] + spread[n_rhs:]
        g[x + 1] = value
        return pack(x, value, carry)

    store_columns(2, lax.fori_loop(0, rows, prolong, empty, unroll=16))
    third = exchange(2, g)

    def post(x):
        cur, total = neighbours(g, x)
        return b[x + 1] + (1.0 - OMEGA) * cur + total

    store_columns(3, sweep(2, third, post, h, 1, 8))
    fourth = exchange(3, h)

    def final(x):
        cur, total = neighbours(h, x)
        return b[x + 1] + (1.0 - OMEGA) * cur + total

    sweep(3, fourth, final, out_ref, 0, 8)
    for copy in started:
        copy.wait_send()


def local(right_side, diagonal, face_weight, aggregation):
    n_group, n_member = lax.axis_size("group"), lax.axis_size("member")
    n_rhs, rows, width = right_side.shape
    padded = pltpu.VMEM((rows + 2, n_rhs, width), F32)
    dma = pltpu.SemaphoreType.DMA
    vmem = pl.BlockSpec(memory_space=pltpu.VMEM)
    out = pl.pallas_call(
        functools.partial(cycle_kernel, n_group, n_member),
        out_shape=jax.ShapeDtypeStruct((rows, n_rhs, width), F32),
        in_specs=[pl.BlockSpec(memory_space=pl.ANY), vmem, vmem, vmem],
        out_specs=vmem,
        scratch_shapes=[
            pltpu.VMEM((rows, n_rhs, width), F32),
            pltpu.VMEM((PLANES, rows, width), F32),
            pltpu.VMEM((rows, AGG, width), BF16),
            pltpu.VMEM((2 * AGG + 16, AGG), F32),
            pltpu.VMEM((8, width), F32),
            pltpu.VMEM((rows, LANES), F32),
            pltpu.VMEM((rows, LANES), jnp.int32),
            pltpu.VMEM((rows, LANES), jnp.int32),
            padded, padded, padded, padded,
            pltpu.VMEM((4, 2, n_rhs, LANES), F32),
            pltpu.VMEM((4, 2, n_rhs, LANES), F32),
            pltpu.VMEM((n_rhs, AGG), F32),
            pltpu.VMEM((len(FAR), n_rhs, AGG), F32),
            pltpu.VMEM((8, AGG), F32),
            pltpu.VMEM((n_member - 1, 8, AGG), F32),
            pltpu.VMEM((3 * AGG, AGG), F32),
            pltpu.VMEM((len(NEAR), 3 * AGG, AGG), F32),
            pltpu.VMEM((2, n_rhs, AGG), F32),
            pltpu.VMEM((len(NEAR), 2, n_rhs, AGG), F32),
            dma((rows,)), dma((len(NEAR),)), dma((len(NEAR),)),
            dma((len(NEAR),)), dma((len(NEAR),)), dma((4,)), dma((4,)),
            dma((4, 4)), dma((4, 4)),
            dma((len(FAR),)), dma((len(FAR),)),
            dma((n_member - 1,)), dma((n_member - 1,)),
        ],
        compiler_params=pltpu.CompilerParams(
            collective_id=0, has_side_effects=True, vmem_limit_bytes=48 * 1024 * 1024
        ),
    )(right_side, diagonal, face_weight, aggregation)
    return out.transpose(1, 0, 2)


def solution(mesh):
    placed = (
        P(None, "group", "member"),
        P("group", "member"),
        P(None, "group", "member"),
        P("group", "member"),
    )
    return jax.shard_map(
        local, mesh=mesh, in_specs=placed, out_specs=P(None, "group", "member"), check_vma=False
    )
```

```python
import functools

import jax
import jax.numpy as jnp
from jax import lax
from jax.experimental import pallas as pl
from jax.experimental.pallas import tpu as pltpu
from jax.sharding import PartitionSpec as P

AGG = 128
POST = 2
CHEB = 6
OMEGA = 0.8
RATIO = 30.0
LANES = 128
MESH = pl.DeviceIdType.MESH
F32 = jnp.float32
BF16 = jnp.bfloat16
NT = (((1,), (1,)), ((), ()))


def split(value):
    high = value.astype(BF16)
    return high, (value - high.astype(F32)).astype(BF16)


AX, AX_LOW, AY, AY_LOW = range(4)
SIDES = 4
Q, Q_INV = 4, 5
LABEL, LABEL_X, LABEL_Y, X_HIGH, X_LOW, Y_HIGH, Y_LOW, G_HIGH, G_LOW = range(6, 15)
PLANES = 15
D_BLOCK = 16
STEP = 8
DEPTH = 3
VEC_REACH = CHEB - 1
MAT_REACH = CHEB - 2


def lanes_of(n_rhs):
    return lax.broadcasted_iota(jnp.int32, (n_rhs, LANES), 1)


def neighbours(buf, co, x, tile):
    rows, n_rhs, width = buf.shape[0] - 2, buf.shape[1], buf.shape[2]
    tiles = width // LANES
    lane = lanes_of(n_rhs)
    cur = buf[x + 1]
    parts = [cur[:, k * LANES:(k + 1) * LANES] for k in range(tiles)]
    if tile is None:
        before = after = jnp.zeros((n_rhs, LANES), F32)
    else:
        before = pltpu.roll(tile, lax.rem(LANES - x, LANES), 1)
        after = pltpu.roll(tile, LANES - 1 - rows - x, 1)
    right = [before] + [pltpu.roll(p, 1, 1) for p in parts]
    left = [pltpu.roll(p, LANES - 1, 1) for p in parts] + [after]
    low = [jnp.where(lane == 0, right[k], right[k + 1]) for k in range(tiles)]
    high = [jnp.where(lane == LANES - 1, left[k + 1], left[k]) for k in range(tiles)]
    low = jnp.concatenate(low, axis=1)
    high = jnp.concatenate(high, axis=1)
    at = pl.ds(x, 1)
    total = co[AX, at, :] * buf[x + 2] + co[AX_LOW, at, :] * buf[x]
    return cur, total + co[AY, at, :] * high + co[AY_LOW, at, :] * low


def final_kernel(h, b, co, side, out_hbm, out, sem):
    rows = out.shape[0]
    tile = side[...]

    def copy(x):
        return pltpu.make_async_copy(out.at[x], out_hbm.at[:, x, :], sem.at[x])

    def step(t, carry):
        for i in range(STEP):
            x = t * STEP + i
            cur, total = neighbours(h, co, x, tile)
            out[x] = b[x + 1] + (1.0 - OMEGA) * cur + total
        for i in range(STEP):
            copy(t * STEP + i).start()
        return carry

    def wait(x, carry):
        copy(x).wait()
        return carry

    lax.fori_loop(0, rows // STEP, step, 0)
    lax.fori_loop(0, rows, wait, 0)


def cycle_kernel(
    n_group, n_member, rhs_hbm, diag_hbm, face_hbm, agg_hbm, h, b, co, side,
    rhs, cf, hot, acc, diag_ref, face_ref, agg_ref, low_row_ref, below_w_ref, below_a_ref, above_a_ref,
    f, g, col_send, col_recv, vec, lm_send, lm_recv, mat, blocks_w,
    rhs_sem, in_sem, edge_ssem, edge_rsem, halo_ssem, halo_rsem, vec_ssem, vec_rsem, mat_ssem, mat_rsem, lm_ssem, lm_rsem,
):
    rows, n_rhs, width = rhs.shape
    gi = lax.axis_index("group")
    mi = lax.axis_index("member")
    g_up, g_down = lax.rem(gi + 1, n_group), lax.rem(gi + n_group - 1, n_group)
    m_up, m_down = lax.rem(mi + 1, n_member), lax.rem(mi + n_member - 1, n_member)

    def is_member(off):
        return (mi + off >= 0) & (mi + off < n_member)

    def fetch(x):
        return pltpu.make_async_copy(rhs_hbm.at[:, x, :], rhs.at[x], rhs_sem.at[x])

    def start_fetch(x, carry):
        fetch(x).start()
        return carry

    loads = [
        pltpu.make_async_copy(src, dst, in_sem.at[i])
        for i, (src, dst) in enumerate((
            (face_hbm, face_ref), (diag_hbm, diag_ref), (agg_hbm, agg_ref)
        ))
    ]
    for load in loads:
        load.start()
    lax.fori_loop(0, rows, start_fetch, 0)

    vec[...] = jnp.zeros_like(vec)
    mat[...] = jnp.zeros_like(mat)
    col_recv[...] = jnp.zeros_like(col_recv)
    for buf in (b, f, g, h):
        buf[0] = jnp.zeros(buf.shape[1:], F32)
        buf[rows + 1] = jnp.zeros(buf.shape[1:], F32)
    barrier = pltpu.get_barrier_semaphore()
    for peer in (g_up, g_down):
        pl.semaphore_signal(barrier, inc=1, device_id=(peer, mi), device_id_type=MESH)
    for off in range(1, n_member):
        peer = lax.rem(mi + off, n_member)
        pl.semaphore_signal(barrier, inc=1, device_id=(gi, peer), device_id_type=MESH)

    lane = lanes_of(n_rhs)
    label = lax.broadcasted_iota(jnp.int32, (AGG, width), 0).astype(F32).astype(BF16)
    one, none = jnp.ones((), BF16), jnp.zeros((), BF16)

    def remote(src, dst, ssem, rsem, target):
        return pltpu.make_async_remote_copy(
            src_ref=src, dst_ref=dst, send_sem=ssem, recv_sem=rsem,
            device_id=target, device_id_type=MESH,
        )

    can_up, can_down = gi < n_group - 1, gi > 0

    def exchange(phase, buf, tile):
        col_send[phase] = tile
        plan = (
            (buf.at[rows], buf.at[0], (g_up, mi), can_up, can_down),
            (buf.at[1], buf.at[rows + 1], (g_down, mi), can_down, can_up),
            (col_send.at[phase], col_recv.at[phase, 0], (gi, m_up), is_member(1), is_member(-1)),
            (col_send.at[phase], col_recv.at[phase, 1], (gi, m_down), is_member(-1), is_member(1)),
        )
        copies = []
        for i, (src, dst, target, sends, gets) in enumerate(plan):
            copy = remote(src, dst, halo_ssem.at[phase, i], halo_rsem.at[phase, i], target)
            pl.when(sends)(copy.start)
            copies.append((sends, gets, copy))
        return copies

    def halo(phase, copies):
        for _, gets, copy in copies:
            pl.when(gets)(copy.wait_recv)
        partial.extend((sends, copy) for sends, _, copy in copies)
        both = jnp.where(lane >= rows, col_recv[phase, 0], col_recv[phase, 1])
        return pltpu.roll(both, rows, 1)

    started = []

    def finish(copies):
        for copy in copies:
            copy.wait_recv()
        started.extend(copies)

    def spread_to(buf, ssem, rsem):
        reach = buf.shape[0] // 2
        copies = []
        for off in range(-reach, reach + 1):
            if off != 0:
                target = lax.rem(mi + off + 2 * n_member, n_member)
                copies.append((off, remote(
                    buf.at[reach], buf.at[reach - off], ssem.at[reach + off], rsem.at[reach - off], (gi, target)
                )))
        for off, copy in copies:
            pl.when(is_member(off))(copy.start)
        return copies

    partial = []

    def collect(copies):
        for off, copy in copies:
            pl.when(is_member(-off))(copy.wait_recv)
        partial.extend((is_member(off), copy) for off, copy in copies)

    def turn(value, shift):
        return pltpu.roll(value, shift % LANES, 1) if shift % LANES else value

    def along_x(buf, tile, j):
        first, last = buf[0], buf[rows + 1]
        down, up = turn(tile, 1), turn(tile, -1)
        down = jnp.where(lane == 0, turn(first[:, :LANES], -j), down)
        down = jnp.where(lane == rows, turn(first[:, width - LANES:], rows + 1 + j), down)
        up = jnp.where(lane == rows - 1, turn(last[:, :LANES], rows - 1 - j), up)
        up = jnp.where(lane == LANES - 1, turn(last[:, width - LANES:], j), up)
        return up, down

    def flip(plane):
        return jnp.concatenate([plane[:, :LANES], plane[:, width - LANES:]], axis=0).T

    at_left = lax.broadcasted_iota(jnp.int32, (1, LANES), 1) < rows

    def pick(left, right, j):
        return jnp.where(at_left, left[j:j + 1], right[LANES - 1 - j:LANES - j])

    def row(plane, x):
        return cf[plane - SIDES, pl.ds(x, 1), :]

    def narrow(plane, x):
        return jnp.broadcast_to(row(plane, x), (16, width)).astype(BF16)

    def spread_row(plane, x):
        return jnp.concatenate([narrow(plane, x)] * (AGG // 16), axis=0)

    for load in loads:
        load.wait()
    wx, wy, agg = face_ref[0], face_ref[1], agg_ref[...].astype(F32)
    xs = lax.broadcasted_iota(jnp.int32, (rows, width), 0)
    ys = lax.broadcasted_iota(jnp.int32, (rows, width), 1)
    wx_low = jnp.where(xs == 0, 0.0, pltpu.roll(wx, 1, 0))
    wy_low = jnp.where(ys == 0, 0.0, pltpu.roll(wy, 1, 1))
    own_diag = diag_ref[...] + wx + wy + wx_low + wy_low
    cf[LABEL - SIDES] = agg
    cf[LABEL_X - SIDES] = pltpu.roll(agg, rows - 1, 0)
    cf[LABEL_Y - SIDES] = pltpu.roll(agg, width - 1, 1)
    inner_y = jnp.where(ys == width - 1, 0.0, wy)
    inner_x = jnp.where(xs == rows - 1, 0.0, wx)
    inner_x = inner_x + jnp.where(cf[LABEL_X - SIDES] == cf[LABEL_Y - SIDES], inner_y, 0.0)
    for plane, value in ((X_HIGH, inner_x), (Y_HIGH, inner_y), (G_HIGH, own_diag)):
        high = value.astype(BF16).astype(F32)
        cf[plane - SIDES] = high
        cf[plane + 1 - SIDES] = value - high
    acc[...] = jnp.zeros_like(acc)

    upper = lax.broadcasted_iota(jnp.int32, (16, width), 0) < 8

    def pairs(block, carry):
        def one_row(i, total):
            x = block * D_BLOCK + i
            own = jnp.where(label == spread_row(LABEL, x), one, none)
            hot[x] = own
            at_x = label == spread_row(LABEL_X, x)
            at_y = label == spread_row(LABEL_Y, x)
            high = jnp.where(at_y, spread_row(Y_HIGH, x), none)
            high = jnp.where(at_x, spread_row(X_HIGH, x), high)
            low = jnp.where(at_y, spread_row(Y_LOW, x), none)
            low = jnp.where(at_x, spread_row(X_LOW, x), low)
            gain = jnp.where(upper, row(G_HIGH, x), row(G_LOW, x)).astype(BF16)
            both = jnp.concatenate([high, low, gain], axis=0)
            return total + lax.dot_general(both, own, NT, preferred_element_type=F32)

        acc[...] += lax.fori_loop(
            0, D_BLOCK, one_row, jnp.zeros(acc.shape, F32), unroll=D_BLOCK
        )
        return carry

    blocks = rows // D_BLOCK
    early = blocks // 2
    lax.fori_loop(0, early, pairs, 0)
    pl.semaphore_wait(barrier, n_member + 1)
    edges = [
        remote(s, d, edge_ssem.at[i], edge_rsem.at[i], t)
        for i, (s, d, t) in enumerate((
            (face_ref.at[0, pl.ds(rows - 8, 8), :], low_row_ref, (g_up, mi)),
            (face_ref.at[1, :, pl.ds(width - LANES, LANES)], below_w_ref, (gi, m_up)),
            (agg_ref.at[:, pl.ds(width - LANES, LANES)], below_a_ref, (gi, m_up)),
            (agg_ref.at[:, pl.ds(0, LANES)], above_a_ref, (gi, m_down)),
        ))
    ]
    for copy in edges:
        copy.start()


    def pack(t, carry):
        for i in range(STEP):
            fetch(t * STEP + i).wait()
        for i in range(STEP):
            x = t * STEP + i
            value = rhs[x]
            left = pltpu.roll(value[:, :LANES], x, 1)
            right = pltpu.roll(value[:, width - LANES:], lax.rem(rows + 1 + x, LANES), 1)
            carry = tuple(
                (jnp.where(lane == x + j, left, a), jnp.where(lane == rows + x - j, right, c))
                for j, (a, c) in enumerate(carry)
            )
        return carry

    blank = jnp.zeros((n_rhs, LANES), F32)
    packed = lax.fori_loop(0, rows // STEP, pack, ((blank, blank),) * DEPTH)
    packed = [
        jnp.where(lane < rows, turn(a, -j), turn(c, j)) for j, (a, c) in enumerate(packed)
    ]
    lax.fori_loop(early, blocks, pairs, 0)
    finish(edges)

    low_row = jnp.where(gi > 0, low_row_ref[7:8, :], 0.0)
    below = jnp.where(mi > 0, below_w_ref[:, LANES - 1:], 0.0)
    wx_low = wx_low + jnp.where(xs == 0, low_row, 0.0)
    wy_low = wy_low + jnp.where(ys == 0, below, 0.0)
    diagf = diag_ref[...] + wx + wy + wx_low + wy_low
    q = OMEGA / diagf
    last_x = (xs == rows - 1) & (gi == n_group - 1)
    last_y = (ys == width - 1) & (mi == n_member - 1)
    co[AX] = jnp.where(last_x, 0.0, q * wx)
    co[AX_LOW] = q * wx_low
    co[AY] = jnp.where(last_y, 0.0, q * wy)
    co[AY_LOW] = q * wy_low
    cf[Q - SIDES] = q
    cf[Q_INV - SIDES] = diagf * (1.0 / OMEGA)

    def scale(x, carry):
        b[x + 1] = rhs[x] * row(Q, x)
        return carry

    scale(0, 0)
    scale(rows - 1, 0)
    q_side = flip(q)
    b_cols = [pick(q_side, q_side, j) * packed[j] for j in range(DEPTH)]
    first = exchange(0, b, b_cols[0])
    lax.fori_loop(1, rows - 1, scale, 0, unroll=8)

    def dot_high(left, right):
        return jnp.dot(
            left, right, precision=lax.Precision.HIGHEST, preferred_element_type=F32
        )

    lab = lax.broadcasted_iota(jnp.int32, (rows, LANES), 1)

    def hot_column(column):
        return jnp.where(column == lab, 1.0, 0.0)

    first_hot = hot_column(agg_ref[:, 0:1])
    last_hot = hot_column(agg_ref[:, width - 1:])
    above = jnp.where(mi < n_member - 1, face_ref[1, :, width - 1:], 0.0)
    first_sum = jnp.sum(first_hot * below, axis=0, keepdims=True)
    last_sum = jnp.sum(last_hot * above, axis=0, keepdims=True)
    low_sum = jnp.sum(hot[0].astype(F32) * low_row, axis=1, keepdims=True)
    eye = lax.broadcasted_iota(jnp.int32, (AGG, AGG), 0)
    eye = eye == lax.broadcasted_iota(jnp.int32, (AGG, AGG), 1)
    gain = acc[2 * AGG:2 * AGG + 1] + acc[2 * AGG + 8:2 * AGG + 9]
    half = jnp.where(eye, 0.5 * (low_sum + gain + first_sum), 0.0)
    half = half - acc[:AGG] - acc[AGG:2 * AGG]
    d_block = half + half.T
    table = jnp.zeros((rows, LANES), F32)
    for i, column in enumerate((
        agg_ref[:, 0:1], below_a_ref[:, LANES - 1:], below,
        agg_ref[:, width - 1:], above_a_ref[:, 0:1], above,
    )):
        table = jnp.where(lab == i, column.astype(F32), table)
    mat[MAT_REACH, :AGG] = d_block
    mat[MAT_REACH, AGG:, :rows] = table.T[:8]
    lm = jnp.sum(jnp.abs(d_block), axis=0, keepdims=True) + first_sum + last_sum
    lm_send[...] = jnp.broadcast_to(lm, lm_send.shape)
    lm_copies = []
    for off in range(1, n_member):
        peer = lax.rem(mi + off, n_member)
        copy = remote(
            lm_send, lm_recv.at[off - 1], lm_ssem.at[off - 1], lm_rsem.at[off - 1], (gi, peer)
        )
        copy.start()
        lm_copies.append(copy)
    ax_side, ax_low_side = flip(co[AX]), flip(co[AX_LOW])
    ay_side, ay_low_side = flip(co[AY]), flip(co[AY_LOW])
    agg_side = flip(cf[LABEL - SIDES])

    def column(buf, tile, cols, j):
        up, down = along_x(buf, cols[j], j)
        total = pick(ax_side, ax_side, j) * up + pick(ax_low_side, ax_low_side, j) * down
        outer = cols[j - 1] if j else tile
        total = total + pick(ay_side, ay_low_side, j) * cols[j + 1]
        return total + pick(ay_low_side, ay_side, j) * outer

    tile = halo(0, first)

    def pre(x, carry):
        cur, total = neighbours(b, co, x, tile)
        f[x + 1] = (2.0 - OMEGA) * cur + total
        return carry

    pre(0, 0)
    pre(rows - 1, 0)
    f_cols = [
        (2.0 - OMEGA) * b_cols[j] + column(b, tile, b_cols, j) for j in range(DEPTH - 1)
    ]
    second = exchange(1, f, f_cols[0])
    mats = spread_to(mat, mat_ssem, mat_rsem)
    lax.fori_loop(1, rows - 1, pre, 0, unroll=8)

    def restrict(x, carry):
        cur, total = neighbours(f, co, x, None)
        resid = (b[x + 1] - OMEGA * cur + total) * row(Q_INV, x)
        high, low = split(resid)
        both = jnp.concatenate([high, low], axis=0)
        return carry + lax.dot_general(both, hot[x], NT, preferred_element_type=F32)

    tile = halo(1, second)
    sums = lax.fori_loop(
        0, rows, restrict, jnp.zeros((2 * n_rhs, AGG), F32), unroll=16
    )
    resid = sums[:n_rhs] + sums[n_rhs:]
    ends = jnp.concatenate([first_hot * below, last_hot * above], axis=0)
    resid = resid + dot_high(tile, ends)

    vec[VEC_REACH] = resid
    vecs = spread_to(vec, vec_ssem, vec_rsem)

    finish(lm_copies)
    lm8 = lm_send[...]
    for off in range(1, n_member):
        lm8 = jnp.maximum(lm8, lm_recv[off - 1])
    lmax = jnp.max(lm8[0:1], axis=1, keepdims=True)
    lmin = lmax / RATIO
    theta = (lmax + lmin) / 2.0
    delta = (lmax - lmin) / 2.0
    sigma = theta / delta
    rho = 1.0 / sigma
    collect(mats)
    place = lax.broadcasted_iota(jnp.int32, (AGG, LANES), 0).astype(F32)

    def couple(source, own, weight):
        value = jnp.where(place == own, weight, 0.0)
        both = jnp.concatenate(split(value), axis=0)
        hot_in = jnp.where(place == source, 1.0, 0.0).astype(BF16)
        prod = lax.dot_general(hot_in, both, NT, preferred_element_type=F32)
        return -(prod[:, :AGG] + prod[:, AGG:])

    for i in range(2 * MAT_REACH + 1):
        line = mat[i, AGG:]
        parts = (
            mat[i, :AGG],
            couple(line[1:2], line[0:1], line[2:3]),
            couple(line[4:5], line[3:4], line[5:6]),
        )
        for k, part in enumerate(parts):
            blocks_w[i, k * AGG:(k + 1) * AGG, :] = jnp.concatenate(split(part), axis=1)

    def product(at, dirs):
        column = jnp.concatenate([dirs[at], dirs[at - 1], dirs[at + 1]], axis=1)
        both = jnp.concatenate(split(column), axis=0)
        prod = jnp.dot(both, blocks_w[at + MAT_REACH], preferred_element_type=F32)
        prod = prod[:n_rhs] + prod[n_rhs:]
        return prod[:, :AGG] + prod[:, AGG:]

    collect(vecs)
    reach = VEC_REACH
    res = {at: vec[at + reach] for at in range(-reach, reach + 1)}
    dirs = {at: value / theta for at, value in res.items()}
    sol = jnp.zeros_like(resid)
    for step in range(CHEB):
        sol = sol + dirs[0]
        if step + 1 < CHEB:
            reach -= 1
            rho_new = 1.0 / (2.0 * sigma - rho)
            own_scale, res_scale = rho_new * rho, 2.0 * rho_new / delta
            inside = range(-reach, reach + 1)
            res = {at: res[at] - product(at, dirs) for at in inside}
            dirs = {at: own_scale * dirs[at] + res_scale * res[at] for at in inside}
            rho = rho_new

    e_high, e_low = split(sol)
    e_both = jnp.concatenate([e_high, e_low], axis=0)

    def prolong(x, carry):
        spread = jnp.dot(e_both, hot[x], preferred_element_type=F32)
        g[x + 1] = f[x + 1] + spread[:n_rhs] + spread[n_rhs:]
        return carry

    def prolong_column(j):
        hot_side = jnp.where(place == pick(agg_side, agg_side, j), 1.0, 0.0).astype(BF16)
        spread = jnp.dot(e_both, hot_side, preferred_element_type=F32)
        return f_cols[j] + spread[:n_rhs] + spread[n_rhs:]

    prolong(0, 0)
    prolong(rows - 1, 0)
    g_cols = [prolong_column(j) for j in range(DEPTH - 1)]
    third = exchange(2, g, g_cols[0])
    lax.fori_loop(1, rows - 1, prolong, 0, unroll=16)
    tile = halo(2, third)

    def post(x, carry):
        cur, total = neighbours(g, co, x, tile)
        h[x + 1] = b[x + 1] + (1.0 - OMEGA) * cur + total
        return carry

    post(0, 0)
    post(rows - 1, 0)
    h_col = b_cols[0] + (1.0 - OMEGA) * g_cols[0] + column(g, tile, g_cols, 0)
    fourth = exchange(3, h, h_col)
    lax.fori_loop(1, rows - 1, post, 0, unroll=8)
    side[...] = halo(3, fourth)
    for copy in started:
        copy.wait_send()
    for sends, copy in partial:
        pl.when(sends)(copy.wait_send)


def local(right_side, diagonal, face_weight, aggregation):
    n_group, n_member = lax.axis_size("group"), lax.axis_size("member")
    n_rhs, rows, width = right_side.shape
    n_vec, n_mat = 2 * VEC_REACH + 1, 2 * MAT_REACH + 1
    padded = pltpu.VMEM((rows + 2, n_rhs, width), F32)
    dma = pltpu.SemaphoreType.DMA
    vmem = pl.BlockSpec(memory_space=pltpu.VMEM)
    strip = pltpu.VMEM((rows, LANES), jnp.int32)
    h, b, co, side = pl.pallas_call(
        functools.partial(cycle_kernel, n_group, n_member),
        out_shape=[
            jax.ShapeDtypeStruct(shape, F32)
            for shape in (
                (rows + 2, n_rhs, width), (rows + 2, n_rhs, width), (SIDES, rows, width), (n_rhs, LANES)
            )
        ],
        in_specs=[pl.BlockSpec(memory_space=pl.ANY)] * 4,
        out_specs=[vmem] * 4,
        scratch_shapes=[
            pltpu.VMEM((rows, n_rhs, width), F32),
            pltpu.VMEM((PLANES - SIDES, rows, width), F32),
            pltpu.VMEM((rows, AGG, width), BF16),
            pltpu.VMEM((2 * AGG + 16, AGG), F32),
            pltpu.VMEM((rows, width), F32),
            pltpu.VMEM((2, rows, width), F32),
            pltpu.VMEM((rows, width), jnp.int32),
            pltpu.VMEM((8, width), F32),
            pltpu.VMEM((rows, LANES), F32),
            strip, strip,
            padded, padded,
            pltpu.VMEM((4, n_rhs, LANES), F32),
            pltpu.VMEM((4, 2, n_rhs, LANES), F32),
            pltpu.VMEM((n_vec, n_rhs, AGG), F32),
            pltpu.VMEM((8, AGG), F32),
            pltpu.VMEM((n_member - 1, 8, AGG), F32),
            pltpu.VMEM((n_mat, AGG + 8, AGG), F32),
            pltpu.VMEM((n_mat, 3 * AGG, 2 * AGG), BF16),
            dma((rows,)), dma((3,)), dma((4,)), dma((4,)), dma((4, 4)), dma((4, 4)),
            dma((n_vec,)), dma((n_vec,)), dma((n_mat,)), dma((n_mat,)),
            dma((n_member - 1,)), dma((n_member - 1,)),
        ],
        compiler_params=pltpu.CompilerParams(
            collective_id=0, has_side_effects=True, vmem_limit_bytes=40 * 1024 * 1024
        ),
    )(*(
        pltpu.with_memory_space_constraint(x, pltpu.HBM)
        for x in (right_side, diagonal, face_weight, aggregation)
    ))
    return pl.pallas_call(
        final_kernel,
        out_shape=jax.ShapeDtypeStruct(right_side.shape, F32),
        in_specs=[vmem] * 4,
        out_specs=pl.BlockSpec(memory_space=pl.ANY),
        scratch_shapes=[pltpu.VMEM((rows, n_rhs, width), F32), dma((rows,))],
        compiler_params=pltpu.CompilerParams(vmem_limit_bytes=16 * 1024 * 1024),
    )(h, b, co, side)


def solution(mesh):
    placed = (
        P(None, "group", "member"),
        P("group", "member"),
        P(None, "group", "member"),
        P("group", "member"),
    )
    return jax.shard_map(
        local, mesh=mesh, in_specs=placed, out_specs=P(None, "group", "member"), check_vma=False
    )
```

```python
import functools

import jax
import jax.numpy as jnp
from jax import lax
from jax.experimental import pallas as pl
from jax.experimental.pallas import tpu as pltpu
from jax.sharding import PartitionSpec as P

AGG = 128
POST = 2
CHEB = 6
OMEGA = 0.8
RATIO = 30.0
LANES = 128
MESH = pl.DeviceIdType.MESH
F32 = jnp.float32
BF16 = jnp.bfloat16
NT = (((1,), (1,)), ((), ()))


def split(value):
    high = value.astype(BF16)
    return high, (value - high.astype(F32)).astype(BF16)


AX, AX_LOW, AY, AY_LOW = range(4)
SIDES = 4
Q, Q_INV = 4, 5
LABEL, LABEL_X, LABEL_Y, X_HIGH, X_LOW, Y_HIGH, Y_LOW, G_HIGH, G_LOW = range(6, 15)
PLANES = 15
D_BLOCK = 16
STEP = 16
DEPTH = 3
VEC_REACH = CHEB - 1
MAT_REACH = CHEB - 2


def lanes_of(n_rhs):
    return lax.broadcasted_iota(jnp.int32, (n_rhs, LANES), 1)


def neighbours(buf, co, x, tile):
    rows, n_rhs, width = buf.shape[0] - 2, buf.shape[1], buf.shape[2]
    tiles = width // LANES
    lane = lanes_of(n_rhs)
    cur = buf[x + 1]
    parts = [cur[:, k * LANES:(k + 1) * LANES] for k in range(tiles)]
    if tile is None:
        before = after = jnp.zeros((n_rhs, LANES), F32)
    else:
        before = pltpu.roll(tile, lax.rem(LANES - x, LANES), 1)
        after = pltpu.roll(tile, LANES - 1 - rows - x, 1)
    right = [before] + [pltpu.roll(p, 1, 1) for p in parts]
    left = [pltpu.roll(p, LANES - 1, 1) for p in parts] + [after]
    low = [jnp.where(lane == 0, right[k], right[k + 1]) for k in range(tiles)]
    high = [jnp.where(lane == LANES - 1, left[k + 1], left[k]) for k in range(tiles)]
    low = jnp.concatenate(low, axis=1)
    high = jnp.concatenate(high, axis=1)
    at = pl.ds(x, 1)
    total = co[AX, at, :] * buf[x + 2] + co[AX_LOW, at, :] * buf[x]
    return cur, total + co[AY, at, :] * high + co[AY_LOW, at, :] * low


def final_kernel(h, b, co, side, out_hbm, out, sem):
    rows = out.shape[0]
    tile = side[...]

    def copy(x):
        return pltpu.make_async_copy(out.at[x], out_hbm.at[:, x, :], sem.at[x])

    def step(t, carry):
        for i in range(STEP):
            x = t * STEP + i
            cur, total = neighbours(h, co, x, tile)
            out[x] = b[x + 1] + (1.0 - OMEGA) * cur + total
        for i in range(STEP):
            copy(t * STEP + i).start()
        return carry

    def wait(x, carry):
        copy(x).wait()
        return carry

    lax.fori_loop(0, rows // STEP, step, 0)
    lax.fori_loop(0, rows, wait, 0)


def cycle_kernel(
    n_group, n_member, rhs_hbm, diag_hbm, face_hbm, agg_hbm, h, b, co, side,
    rhs, cf, hot, acc, diag_ref, face_ref, agg_ref, low_row_ref, below_w_ref, below_a_ref, above_a_ref,
    f, g, col_send, col_recv, vec, lm_send, lm_recv, mat, blocks_w,
    rhs_sem, in_sem, edge_ssem, edge_rsem, halo_ssem, halo_rsem, vec_ssem, vec_rsem, mat_ssem, mat_rsem, lm_ssem, lm_rsem,
):
    rows, n_rhs, width = rhs.shape
    gi = lax.axis_index("group")
    mi = lax.axis_index("member")
    g_up, g_down = lax.rem(gi + 1, n_group), lax.rem(gi + n_group - 1, n_group)
    m_up, m_down = lax.rem(mi + 1, n_member), lax.rem(mi + n_member - 1, n_member)

    def is_member(off):
        return (mi + off >= 0) & (mi + off < n_member)

    def fetch(x):
        return pltpu.make_async_copy(rhs_hbm.at[:, x, :], rhs.at[x], rhs_sem.at[x])

    def start_fetch(x, carry):
        fetch(x).start()
        return carry

    loads = [
        pltpu.make_async_copy(src, dst, in_sem.at[i])
        for i, (src, dst) in enumerate((
            (face_hbm, face_ref), (diag_hbm, diag_ref), (agg_hbm, agg_ref)
        ))
    ]
    for load in loads:
        load.start()
    lax.fori_loop(0, rows, start_fetch, 0)

    vec[...] = jnp.zeros_like(vec)
    mat[...] = jnp.zeros_like(mat)
    col_recv[...] = jnp.zeros_like(col_recv)
    for buf in (b, f, g, h):
        buf[0] = jnp.zeros(buf.shape[1:], F32)
        buf[rows + 1] = jnp.zeros(buf.shape[1:], F32)
    barrier = pltpu.get_barrier_semaphore()
    for peer in (g_up, g_down):
        pl.semaphore_signal(barrier, inc=1, device_id=(peer, mi), device_id_type=MESH)
    for off in range(1, n_member):
        peer = lax.rem(mi + off, n_member)
        pl.semaphore_signal(barrier, inc=1, device_id=(gi, peer), device_id_type=MESH)

    lane = lanes_of(n_rhs)
    label = lax.broadcasted_iota(jnp.int32, (AGG, width), 0).astype(F32).astype(BF16)
    one, none = jnp.ones((), BF16), jnp.zeros((), BF16)

    def interior(body):
        whole = (rows - 2) // STEP * STEP
        lax.fori_loop(1, 1 + whole, body, 0, unroll=STEP)
        if whole < rows - 2:
            lax.fori_loop(1 + whole, rows - 1, body, 0, unroll=rows - 2 - whole)

    def remote(src, dst, ssem, rsem, target):
        return pltpu.make_async_remote_copy(
            src_ref=src, dst_ref=dst, send_sem=ssem, recv_sem=rsem,
            device_id=target, device_id_type=MESH,
        )

    can_up, can_down = gi < n_group - 1, gi > 0

    def exchange(phase, buf, tile):
        col_send[phase] = tile
        plan = (
            (buf.at[rows], buf.at[0], (g_up, mi), can_up, can_down),
            (buf.at[1], buf.at[rows + 1], (g_down, mi), can_down, can_up),
            (col_send.at[phase], col_recv.at[phase, 0], (gi, m_up), is_member(1), is_member(-1)),
            (col_send.at[phase], col_recv.at[phase, 1], (gi, m_down), is_member(-1), is_member(1)),
        )
        copies = []
        for i, (src, dst, target, sends, gets) in enumerate(plan):
            copy = remote(src, dst, halo_ssem.at[phase, i], halo_rsem.at[phase, i], target)
            pl.when(sends)(copy.start)
            copies.append((sends, gets, copy))
        return copies

    def halo(phase, copies):
        for _, gets, copy in copies:
            pl.when(gets)(copy.wait_recv)
        partial.extend((sends, copy) for sends, _, copy in copies)
        both = jnp.where(lane >= rows, col_recv[phase, 0], col_recv[phase, 1])
        return pltpu.roll(both, rows, 1)

    started = []

    def finish(copies):
        for copy in copies:
            copy.wait_recv()
        started.extend(copies)

    def spread_to(buf, ssem, rsem):
        reach = buf.shape[0] // 2
        copies = []
        for off in range(-reach, reach + 1):
            if off != 0:
                target = lax.rem(mi + off + 2 * n_member, n_member)
                copies.append((off, remote(
                    buf.at[reach], buf.at[reach - off], ssem.at[reach + off], rsem.at[reach - off], (gi, target)
                )))
        for off, copy in copies:
            pl.when(is_member(off))(copy.start)
        return copies

    partial = []

    def collect(copies):
        for off, copy in copies:
            pl.when(is_member(-off))(copy.wait_recv)
        partial.extend((is_member(off), copy) for off, copy in copies)

    def turn(value, shift):
        return pltpu.roll(value, shift % LANES, 1) if shift % LANES else value

    def along_x(buf, tile, j):
        first, last = buf[0], buf[rows + 1]
        down, up = turn(tile, 1), turn(tile, -1)
        down = jnp.where(lane == 0, turn(first[:, :LANES], -j), down)
        down = jnp.where(lane == rows, turn(first[:, width - LANES:], rows + 1 + j), down)
        up = jnp.where(lane == rows - 1, turn(last[:, :LANES], rows - 1 - j), up)
        up = jnp.where(lane == LANES - 1, turn(last[:, width - LANES:], j), up)
        return up, down

    def flip(plane):
        return jnp.concatenate([plane[:, :LANES], plane[:, width - LANES:]], axis=0).T

    at_left = lax.broadcasted_iota(jnp.int32, (1, LANES), 1) < rows

    def pick(left, right, j):
        return jnp.where(at_left, left[j:j + 1], right[LANES - 1 - j:LANES - j])

    def row(plane, x):
        return cf[plane - SIDES, pl.ds(x, 1), :]

    def narrow(plane, x):
        return jnp.broadcast_to(row(plane, x), (16, width)).astype(BF16)

    def spread_row(plane, x):
        return jnp.concatenate([narrow(plane, x)] * (AGG // 16), axis=0)

    for load in loads:
        load.wait()
    wx, wy, agg = face_ref[0], face_ref[1], agg_ref[...].astype(F32)
    xs = lax.broadcasted_iota(jnp.int32, (rows, width), 0)
    ys = lax.broadcasted_iota(jnp.int32, (rows, width), 1)
    wx_low = jnp.where(xs == 0, 0.0, pltpu.roll(wx, 1, 0))
    wy_low = jnp.where(ys == 0, 0.0, pltpu.roll(wy, 1, 1))
    own_diag = diag_ref[...] + wx + wy + wx_low + wy_low
    cf[LABEL - SIDES] = agg
    cf[LABEL_X - SIDES] = pltpu.roll(agg, rows - 1, 0)
    cf[LABEL_Y - SIDES] = pltpu.roll(agg, width - 1, 1)
    inner_y = jnp.where(ys == width - 1, 0.0, wy)
    inner_x = jnp.where(xs == rows - 1, 0.0, wx)
    inner_x = inner_x + jnp.where(cf[LABEL_X - SIDES] == cf[LABEL_Y - SIDES], inner_y, 0.0)
    for plane, value in ((X_HIGH, inner_x), (Y_HIGH, inner_y), (G_HIGH, own_diag)):
        high = value.astype(BF16).astype(F32)
        cf[plane - SIDES] = high
        cf[plane + 1 - SIDES] = value - high
    acc[...] = jnp.zeros_like(acc)

    upper = lax.broadcasted_iota(jnp.int32, (16, width), 0) < 8

    def pairs(block, carry):
        def one_row(i, total):
            x = block * D_BLOCK + i
            own = jnp.where(label == spread_row(LABEL, x), one, none)
            hot[x] = own
            at_x = label == spread_row(LABEL_X, x)
            at_y = label == spread_row(LABEL_Y, x)
            high = jnp.where(at_y, spread_row(Y_HIGH, x), none)
            high = jnp.where(at_x, spread_row(X_HIGH, x), high)
            low = jnp.where(at_y, spread_row(Y_LOW, x), none)
            low = jnp.where(at_x, spread_row(X_LOW, x), low)
            gain = jnp.where(upper, row(G_HIGH, x), row(G_LOW, x)).astype(BF16)
            both = jnp.concatenate([high, low, gain], axis=0)
            return total + lax.dot_general(both, own, NT, preferred_element_type=F32)

        acc[...] += lax.fori_loop(
            0, D_BLOCK, one_row, jnp.zeros(acc.shape, F32), unroll=D_BLOCK
        )
        return carry

    blocks = rows // D_BLOCK
    early = blocks // 2
    lax.fori_loop(0, early, pairs, 0)
    pl.semaphore_wait(barrier, n_member + 1)
    edges = [
        remote(s, d, edge_ssem.at[i], edge_rsem.at[i], t)
        for i, (s, d, t) in enumerate((
            (face_ref.at[0, pl.ds(rows - 8, 8), :], low_row_ref, (g_up, mi)),
            (face_ref.at[1, :, pl.ds(width - LANES, LANES)], below_w_ref, (gi, m_up)),
            (agg_ref.at[:, pl.ds(width - LANES, LANES)], below_a_ref, (gi, m_up)),
            (agg_ref.at[:, pl.ds(0, LANES)], above_a_ref, (gi, m_down)),
        ))
    ]
    for copy in edges:
        copy.start()


    def pack(t, carry):
        for i in range(STEP):
            fetch(t * STEP + i).wait()
        for i in range(STEP):
            x = t * STEP + i
            value = rhs[x]
            left = pltpu.roll(value[:, :LANES], x, 1)
            right = pltpu.roll(value[:, width - LANES:], lax.rem(rows + 1 + x, LANES), 1)
            carry = tuple(
                (jnp.where(lane == x + j, left, a), jnp.where(lane == rows + x - j, right, c))
                for j, (a, c) in enumerate(carry)
            )
        return carry

    blank = jnp.zeros((n_rhs, LANES), F32)
    packed = lax.fori_loop(0, rows // STEP, pack, ((blank, blank),) * DEPTH)
    packed = [
        jnp.where(lane < rows, turn(a, -j), turn(c, j)) for j, (a, c) in enumerate(packed)
    ]
    lax.fori_loop(early, blocks, pairs, 0)
    finish(edges)

    low_row = jnp.where(gi > 0, low_row_ref[7:8, :], 0.0)
    below = jnp.where(mi > 0, below_w_ref[:, LANES - 1:], 0.0)
    wx_low = wx_low + jnp.where(xs == 0, low_row, 0.0)
    wy_low = wy_low + jnp.where(ys == 0, below, 0.0)
    diagf = diag_ref[...] + wx + wy + wx_low + wy_low
    q = OMEGA / diagf
    last_x = (xs == rows - 1) & (gi == n_group - 1)
    last_y = (ys == width - 1) & (mi == n_member - 1)
    co[AX] = jnp.where(last_x, 0.0, q * wx)
    co[AX_LOW] = q * wx_low
    co[AY] = jnp.where(last_y, 0.0, q * wy)
    co[AY_LOW] = q * wy_low
    cf[Q - SIDES] = q
    cf[Q_INV - SIDES] = diagf * (1.0 / OMEGA)

    def scale(x, carry):
        b[x + 1] = rhs[x] * row(Q, x)
        return carry

    scale(0, 0)
    scale(rows - 1, 0)
    q_side = flip(q)
    b_cols = [pick(q_side, q_side, j) * packed[j] for j in range(DEPTH)]
    first = exchange(0, b, b_cols[0])
    interior(scale)

    def dot_high(left, right):
        return jnp.dot(
            left, right, precision=lax.Precision.HIGHEST, preferred_element_type=F32
        )

    lab = lax.broadcasted_iota(jnp.int32, (rows, LANES), 1)

    def hot_column(column):
        return jnp.where(column == lab, 1.0, 0.0)

    first_hot = hot_column(agg_ref[:, 0:1])
    last_hot = hot_column(agg_ref[:, width - 1:])
    above = jnp.where(mi < n_member - 1, face_ref[1, :, width - 1:], 0.0)
    first_sum = jnp.sum(first_hot * below, axis=0, keepdims=True)
    last_sum = jnp.sum(last_hot * above, axis=0, keepdims=True)
    low_sum = jnp.sum(hot[0].astype(F32) * low_row, axis=1, keepdims=True)
    eye = lax.broadcasted_iota(jnp.int32, (AGG, AGG), 0)
    eye = eye == lax.broadcasted_iota(jnp.int32, (AGG, AGG), 1)
    gain = acc[2 * AGG:2 * AGG + 1] + acc[2 * AGG + 8:2 * AGG + 9]
    half = jnp.where(eye, 0.5 * (low_sum + gain + first_sum), 0.0)
    half = half - acc[:AGG] - acc[AGG:2 * AGG]
    d_block = half + half.T
    table = jnp.zeros((rows, LANES), F32)
    for i, column in enumerate((
        agg_ref[:, 0:1], below_a_ref[:, LANES - 1:], below,
        agg_ref[:, width - 1:], above_a_ref[:, 0:1], above,
    )):
        table = jnp.where(lab == i, column.astype(F32), table)
    mat[MAT_REACH, :AGG] = d_block
    mat[MAT_REACH, AGG:, :rows] = table.T[:8]
    lm = jnp.sum(jnp.abs(d_block), axis=0, keepdims=True) + first_sum + last_sum
    lm_send[...] = jnp.broadcast_to(lm, lm_send.shape)
    lm_copies = []
    for off in range(1, n_member):
        peer = lax.rem(mi + off, n_member)
        copy = remote(
            lm_send, lm_recv.at[off - 1], lm_ssem.at[off - 1], lm_rsem.at[off - 1], (gi, peer)
        )
        copy.start()
        lm_copies.append(copy)
    ax_side, ax_low_side = flip(co[AX]), flip(co[AX_LOW])
    ay_side, ay_low_side = flip(co[AY]), flip(co[AY_LOW])
    agg_side = flip(cf[LABEL - SIDES])

    def column(buf, tile, cols, j):
        up, down = along_x(buf, cols[j], j)
        total = pick(ax_side, ax_side, j) * up + pick(ax_low_side, ax_low_side, j) * down
        outer = cols[j - 1] if j else tile
        total = total + pick(ay_side, ay_low_side, j) * cols[j + 1]
        return total + pick(ay_low_side, ay_side, j) * outer

    tile = halo(0, first)

    def pre(x, carry):
        cur, total = neighbours(b, co, x, tile)
        f[x + 1] = (2.0 - OMEGA) * cur + total
        return carry

    pre(0, 0)
    pre(rows - 1, 0)
    f_cols = [
        (2.0 - OMEGA) * b_cols[j] + column(b, tile, b_cols, j) for j in range(DEPTH - 1)
    ]
    second = exchange(1, f, f_cols[0])
    mats = spread_to(mat, mat_ssem, mat_rsem)
    interior(pre)

    def restrict(x, carry):
        cur, total = neighbours(f, co, x, None)
        resid = (b[x + 1] - OMEGA * cur + total) * row(Q_INV, x)
        high, low = split(resid)
        both = jnp.concatenate([high, low], axis=0)
        return carry + lax.dot_general(both, hot[x], NT, preferred_element_type=F32)

    tile = halo(1, second)
    sums = lax.fori_loop(
        0, rows, restrict, jnp.zeros((2 * n_rhs, AGG), F32), unroll=16
    )
    resid = sums[:n_rhs] + sums[n_rhs:]
    ends = jnp.concatenate([first_hot * below, last_hot * above], axis=0)
    resid = resid + dot_high(tile, ends)

    vec[VEC_REACH] = resid
    vecs = spread_to(vec, vec_ssem, vec_rsem)

    finish(lm_copies)
    lm8 = lm_send[...]
    for off in range(1, n_member):
        lm8 = jnp.maximum(lm8, lm_recv[off - 1])
    lmax = jnp.max(lm8[0:1], axis=1, keepdims=True)
    lmin = lmax / RATIO
    theta = (lmax + lmin) / 2.0
    delta = (lmax - lmin) / 2.0
    sigma = theta / delta
    rho = 1.0 / sigma
    collect(mats)
    place = lax.broadcasted_iota(jnp.int32, (AGG, LANES), 0).astype(F32)

    def couple(source, own, weight):
        value = jnp.where(place == own, weight, 0.0)
        both = jnp.concatenate(split(value), axis=0)
        hot_in = jnp.where(place == source, 1.0, 0.0).astype(BF16)
        prod = lax.dot_general(hot_in, both, NT, preferred_element_type=F32)
        return -(prod[:, :AGG] + prod[:, AGG:])

    for i in range(2 * MAT_REACH + 1):
        line = mat[i, AGG:]
        parts = (
            mat[i, :AGG],
            couple(line[1:2], line[0:1], line[2:3]),
            couple(line[4:5], line[3:4], line[5:6]),
        )
        for k, part in enumerate(parts):
            blocks_w[i, k * AGG:(k + 1) * AGG, :] = jnp.concatenate(split(part), axis=1)

    def product(at, dirs):
        column = jnp.concatenate([dirs[at], dirs[at - 1], dirs[at + 1]], axis=1)
        both = jnp.concatenate(split(column), axis=0)
        prod = jnp.dot(both, blocks_w[at + MAT_REACH], preferred_element_type=F32)
        prod = prod[:n_rhs] + prod[n_rhs:]
        return prod[:, :AGG] + prod[:, AGG:]

    collect(vecs)
    reach = VEC_REACH
    res = {at: vec[at + reach] for at in range(-reach, reach + 1)}
    dirs = {at: value / theta for at, value in res.items()}
    sol = jnp.zeros_like(resid)
    for step in range(CHEB):
        sol = sol + dirs[0]
        if step + 1 < CHEB:
            reach -= 1
            rho_new = 1.0 / (2.0 * sigma - rho)
            own_scale, res_scale = rho_new * rho, 2.0 * rho_new / delta
            inside = range(-reach, reach + 1)
            res = {at: res[at] - product(at, dirs) for at in inside}
            dirs = {at: own_scale * dirs[at] + res_scale * res[at] for at in inside}
            rho = rho_new

    e_high, e_low = split(sol)
    e_both = jnp.concatenate([e_high, e_low], axis=0)

    def prolong(x, carry):
        spread = jnp.dot(e_both, hot[x], preferred_element_type=F32)
        g[x + 1] = f[x + 1] + spread[:n_rhs] + spread[n_rhs:]
        return carry

    def prolong_column(j):
        hot_side = jnp.where(place == pick(agg_side, agg_side, j), 1.0, 0.0).astype(BF16)
        spread = jnp.dot(e_both, hot_side, preferred_element_type=F32)
        return f_cols[j] + spread[:n_rhs] + spread[n_rhs:]

    prolong(0, 0)
    prolong(rows - 1, 0)
    g_cols = [prolong_column(j) for j in range(DEPTH - 1)]
    third = exchange(2, g, g_cols[0])
    interior(prolong)
    tile = halo(2, third)

    def post(x, carry):
        cur, total = neighbours(g, co, x, tile)
        h[x + 1] = b[x + 1] + (1.0 - OMEGA) * cur + total
        return carry

    post(0, 0)
    post(rows - 1, 0)
    h_col = b_cols[0] + (1.0 - OMEGA) * g_cols[0] + column(g, tile, g_cols, 0)
    fourth = exchange(3, h, h_col)
    interior(post)
    side[...] = halo(3, fourth)
    for copy in started:
        copy.wait_send()
    for sends, copy in partial:
        pl.when(sends)(copy.wait_send)


def local(right_side, diagonal, face_weight, aggregation):
    n_group, n_member = lax.axis_size("group"), lax.axis_size("member")
    n_rhs, rows, width = right_side.shape
    n_vec, n_mat = 2 * VEC_REACH + 1, 2 * MAT_REACH + 1
    padded = pltpu.VMEM((rows + 2, n_rhs, width), F32)
    dma = pltpu.SemaphoreType.DMA
    vmem = pl.BlockSpec(memory_space=pltpu.VMEM)
    strip = pltpu.VMEM((rows, LANES), jnp.int32)
    h, b, co, side = pl.pallas_call(
        functools.partial(cycle_kernel, n_group, n_member),
        out_shape=[
            jax.ShapeDtypeStruct(shape, F32)
            for shape in (
                (rows + 2, n_rhs, width), (rows + 2, n_rhs, width), (SIDES, rows, width), (n_rhs, LANES)
            )
        ],
        in_specs=[pl.BlockSpec(memory_space=pl.ANY)] * 4,
        out_specs=[vmem] * 4,
        scratch_shapes=[
            pltpu.VMEM((rows, n_rhs, width), F32),
            pltpu.VMEM((PLANES - SIDES, rows, width), F32),
            pltpu.VMEM((rows, AGG, width), BF16),
            pltpu.VMEM((2 * AGG + 16, AGG), F32),
            pltpu.VMEM((rows, width), F32),
            pltpu.VMEM((2, rows, width), F32),
            pltpu.VMEM((rows, width), jnp.int32),
            pltpu.VMEM((8, width), F32),
            pltpu.VMEM((rows, LANES), F32),
            strip, strip,
            padded, padded,
            pltpu.VMEM((4, n_rhs, LANES), F32),
            pltpu.VMEM((4, 2, n_rhs, LANES), F32),
            pltpu.VMEM((n_vec, n_rhs, AGG), F32),
            pltpu.VMEM((8, AGG), F32),
            pltpu.VMEM((n_member - 1, 8, AGG), F32),
            pltpu.VMEM((n_mat, AGG + 8, AGG), F32),
            pltpu.VMEM((n_mat, 3 * AGG, 2 * AGG), BF16),
            dma((rows,)), dma((3,)), dma((4,)), dma((4,)), dma((4, 4)), dma((4, 4)),
            dma((n_vec,)), dma((n_vec,)), dma((n_mat,)), dma((n_mat,)),
            dma((n_member - 1,)), dma((n_member - 1,)),
        ],
        compiler_params=pltpu.CompilerParams(
            collective_id=0, has_side_effects=True, vmem_limit_bytes=40 * 1024 * 1024
        ),
    )(*(
        pltpu.with_memory_space_constraint(x, pltpu.HBM)
        for x in (right_side, diagonal, face_weight, aggregation)
    ))
    return pl.pallas_call(
        final_kernel,
        out_shape=jax.ShapeDtypeStruct(right_side.shape, F32),
        in_specs=[vmem] * 4,
        out_specs=pl.BlockSpec(memory_space=pl.ANY),
        scratch_shapes=[pltpu.VMEM((rows, n_rhs, width), F32), dma((rows,))],
        compiler_params=pltpu.CompilerParams(vmem_limit_bytes=16 * 1024 * 1024),
    )(h, b, co, side)


def solution(mesh):
    placed = (
        P(None, "group", "member"),
        P("group", "member"),
        P(None, "group", "member"),
        P("group", "member"),
    )
    return jax.shard_map(
        local, mesh=mesh, in_specs=placed, out_specs=P(None, "group", "member"), check_vma=False
    )
```

```python
import functools

import jax
import jax.numpy as jnp
from jax import lax
from jax.experimental import pallas as pl
from jax.experimental.pallas import tpu as pltpu
from jax.sharding import PartitionSpec as P

AGG = 128
POST = 2
CHEB = 6
OMEGA = 0.8
RATIO = 30.0
LANES = 128
MESH = pl.DeviceIdType.MESH
F32 = jnp.float32
BF16 = jnp.bfloat16
NT = (((1,), (1,)), ((), ()))


def split(value):
    high = value.astype(BF16)
    return high, (value - high.astype(F32)).astype(BF16)


AX, AX_LOW, AY, AY_LOW = range(4)
SIDES = 4
Q, Q_INV = 4, 5
LABEL, LABEL_X, LABEL_Y, X_HIGH, X_LOW, Y_HIGH, Y_LOW, G_HIGH, G_LOW = range(6, 15)
PLANES = 15
D_BLOCK = 16
HALF = AGG // 2
STEP = 16
DEPTH = 3
VEC_REACH = CHEB - 1
MAT_REACH = CHEB - 2


def lanes_of(n_rhs):
    return lax.broadcasted_iota(jnp.int32, (n_rhs, LANES), 1)


def neighbours(buf, co, x, tile):
    rows, n_rhs, width = buf.shape[0] - 2, buf.shape[1], buf.shape[2]
    tiles = width // LANES
    lane = lanes_of(n_rhs)
    cur = buf[x + 1]
    parts = [cur[:, k * LANES:(k + 1) * LANES] for k in range(tiles)]
    if tile is None:
        before = after = jnp.zeros((n_rhs, LANES), F32)
    else:
        before = pltpu.roll(tile, lax.rem(LANES - x, LANES), 1)
        after = pltpu.roll(tile, LANES - 1 - rows - x, 1)
    right = [before] + [pltpu.roll(p, 1, 1) for p in parts]
    left = [pltpu.roll(p, LANES - 1, 1) for p in parts] + [after]
    low = [jnp.where(lane == 0, right[k], right[k + 1]) for k in range(tiles)]
    high = [jnp.where(lane == LANES - 1, left[k + 1], left[k]) for k in range(tiles)]
    low = jnp.concatenate(low, axis=1)
    high = jnp.concatenate(high, axis=1)
    at = pl.ds(x, 1)
    total = co[AX, at, :] * buf[x + 2] + co[AX_LOW, at, :] * buf[x]
    return cur, total + co[AY, at, :] * high + co[AY_LOW, at, :] * low


def final_kernel(h, b, co, side, out_hbm, out, sem):
    rows = out.shape[0]
    tile = side[...]

    def copy(x):
        return pltpu.make_async_copy(out.at[x], out_hbm.at[:, x, :], sem.at[x])

    def step(t, carry):
        for i in range(STEP):
            x = t * STEP + i
            cur, total = neighbours(h, co, x, tile)
            out[x] = b[x + 1] + (1.0 - OMEGA) * cur + total
        for i in range(STEP):
            copy(t * STEP + i).start()
        return carry

    def wait(x, carry):
        copy(x).wait()
        return carry

    lax.fori_loop(0, rows // STEP, step, 0)
    lax.fori_loop(0, rows, wait, 0)


def cycle_kernel(
    n_group, n_member, rhs_hbm, diag_hbm, face_hbm, agg_hbm, h, b, co, side,
    rhs, cf, hot, acc, diag_ref, face_ref, agg_ref, low_row_ref, below_w_ref, below_a_ref, above_a_ref,
    f, g, col_send, col_recv, vec, lm_send, lm_recv, mat, blocks_w,
    rhs_sem, in_sem, edge_ssem, edge_rsem, halo_ssem, halo_rsem, vec_ssem, vec_rsem, mat_ssem, mat_rsem, lm_ssem, lm_rsem,
):
    rows, n_rhs, width = rhs.shape
    gi = lax.axis_index("group")
    mi = lax.axis_index("member")
    g_up, g_down = lax.rem(gi + 1, n_group), lax.rem(gi + n_group - 1, n_group)
    m_up, m_down = lax.rem(mi + 1, n_member), lax.rem(mi + n_member - 1, n_member)

    def is_member(off):
        return (mi + off >= 0) & (mi + off < n_member)

    def fetch(x):
        return pltpu.make_async_copy(rhs_hbm.at[:, x, :], rhs.at[x], rhs_sem.at[x])

    def start_fetch(x, carry):
        fetch(x).start()
        return carry

    loads = [
        pltpu.make_async_copy(src, dst, in_sem.at[i])
        for i, (src, dst) in enumerate((
            (face_hbm, face_ref), (diag_hbm, diag_ref), (agg_hbm, agg_ref)
        ))
    ]
    for load in loads:
        load.start()
    lax.fori_loop(0, rows, start_fetch, 0)

    vec[...] = jnp.zeros_like(vec)
    mat[...] = jnp.zeros_like(mat)
    col_recv[...] = jnp.zeros_like(col_recv)
    for buf in (b, f, g, h):
        buf[0] = jnp.zeros(buf.shape[1:], F32)
        buf[rows + 1] = jnp.zeros(buf.shape[1:], F32)
    barrier = pltpu.get_barrier_semaphore()
    for peer in (g_up, g_down):
        pl.semaphore_signal(barrier, inc=1, device_id=(peer, mi), device_id_type=MESH)
    for off in range(1, n_member):
        peer = lax.rem(mi + off, n_member)
        pl.semaphore_signal(barrier, inc=1, device_id=(gi, peer), device_id_type=MESH)

    lane = lanes_of(n_rhs)
    label = lax.broadcasted_iota(jnp.int32, (AGG, width), 0).astype(F32).astype(BF16)
    one, none = jnp.ones((), BF16), jnp.zeros((), BF16)

    def interior(body):
        whole = (rows - 2) // STEP * STEP
        lax.fori_loop(1, 1 + whole, body, 0, unroll=STEP)
        if whole < rows - 2:
            lax.fori_loop(1 + whole, rows - 1, body, 0, unroll=rows - 2 - whole)

    def remote(src, dst, ssem, rsem, target):
        return pltpu.make_async_remote_copy(
            src_ref=src, dst_ref=dst, send_sem=ssem, recv_sem=rsem,
            device_id=target, device_id_type=MESH,
        )

    can_up, can_down = gi < n_group - 1, gi > 0

    def exchange(phase, buf, tile):
        col_send[phase] = tile
        plan = (
            (buf.at[rows], buf.at[0], (g_up, mi), can_up, can_down),
            (buf.at[1], buf.at[rows + 1], (g_down, mi), can_down, can_up),
            (col_send.at[phase], col_recv.at[phase, 0], (gi, m_up), is_member(1), is_member(-1)),
            (col_send.at[phase], col_recv.at[phase, 1], (gi, m_down), is_member(-1), is_member(1)),
        )
        copies = []
        for i, (src, dst, target, sends, gets) in enumerate(plan):
            copy = remote(src, dst, halo_ssem.at[phase, i], halo_rsem.at[phase, i], target)
            pl.when(sends)(copy.start)
            copies.append((sends, gets, copy))
        return copies

    def halo(phase, copies):
        for _, gets, copy in copies:
            pl.when(gets)(copy.wait_recv)
        partial.extend((sends, copy) for sends, _, copy in copies)
        both = jnp.where(lane >= rows, col_recv[phase, 0], col_recv[phase, 1])
        return pltpu.roll(both, rows, 1)

    started = []

    def finish(copies):
        for copy in copies:
            copy.wait_recv()
        started.extend(copies)

    def spread_to(buf, ssem, rsem):
        reach = buf.shape[0] // 2
        copies = []
        for off in sorted(range(-reach, reach + 1), key=lambda o: -abs(o)):
            if off != 0:
                target = lax.rem(mi + off + 2 * n_member, n_member)
                copies.append((off, remote(
                    buf.at[reach], buf.at[reach - off], ssem.at[reach + off], rsem.at[reach - off], (gi, target)
                )))
        for off, copy in copies:
            pl.when(is_member(off))(copy.start)
        return copies

    partial = []

    def collect(copies):
        for off, copy in copies:
            pl.when(is_member(-off))(copy.wait_recv)
        partial.extend((is_member(off), copy) for off, copy in copies)

    def turn(value, shift):
        return pltpu.roll(value, shift % LANES, 1) if shift % LANES else value

    def along_x(buf, tile, j):
        first, last = buf[0], buf[rows + 1]
        down, up = turn(tile, 1), turn(tile, -1)
        down = jnp.where(lane == 0, turn(first[:, :LANES], -j), down)
        down = jnp.where(lane == rows, turn(first[:, width - LANES:], rows + 1 + j), down)
        up = jnp.where(lane == rows - 1, turn(last[:, :LANES], rows - 1 - j), up)
        up = jnp.where(lane == LANES - 1, turn(last[:, width - LANES:], j), up)
        return up, down

    def flip(plane):
        return jnp.concatenate([plane[:, :LANES], plane[:, width - LANES:]], axis=0).T

    at_left = lax.broadcasted_iota(jnp.int32, (1, LANES), 1) < rows

    def pick(left, right, j):
        return jnp.where(at_left, left[j:j + 1], right[LANES - 1 - j:LANES - j])

    def row(plane, x):
        return cf[plane - SIDES, pl.ds(x, 1), :]

    def narrow(plane, x):
        return jnp.broadcast_to(row(plane, x), (16, width)).astype(BF16)

    def spread_row(plane, x):
        return jnp.concatenate([narrow(plane, x)] * (AGG // 16), axis=0)

    for load in loads:
        load.wait()
    wx, wy, agg = face_ref[0], face_ref[1], agg_ref[...].astype(F32)
    xs = lax.broadcasted_iota(jnp.int32, (rows, width), 0)
    ys = lax.broadcasted_iota(jnp.int32, (rows, width), 1)
    wx_low = jnp.where(xs == 0, 0.0, pltpu.roll(wx, 1, 0))
    wy_low = jnp.where(ys == 0, 0.0, pltpu.roll(wy, 1, 1))
    own_diag = diag_ref[...] + wx + wy + wx_low + wy_low
    cf[LABEL - SIDES] = agg
    cf[LABEL_X - SIDES] = pltpu.roll(agg, rows - 1, 0)
    cf[LABEL_Y - SIDES] = pltpu.roll(agg, width - 1, 1)
    inner_y = jnp.where(ys == width - 1, 0.0, wy)
    inner_x = jnp.where(xs == rows - 1, 0.0, wx)
    inner_x = inner_x + jnp.where(cf[LABEL_X - SIDES] == cf[LABEL_Y - SIDES], inner_y, 0.0)
    for plane, value in ((X_HIGH, inner_x), (Y_HIGH, inner_y), (G_HIGH, own_diag)):
        high = value.astype(BF16).astype(F32)
        cf[plane - SIDES] = high
        cf[plane + 1 - SIDES] = value - high
    acc[...] = jnp.zeros_like(acc)

    upper = lax.broadcasted_iota(jnp.int32, (16, width), 0) < 8

    def pairs(block, carry):
        def one_row(i, total):
            x = block * D_BLOCK + i
            own = jnp.where(label == spread_row(LABEL, x), one, none)
            hot[x] = own
            at_x = label == spread_row(LABEL_X, x)
            at_y = label == spread_row(LABEL_Y, x)
            high = jnp.where(at_y, spread_row(Y_HIGH, x), none)
            high = jnp.where(at_x, spread_row(X_HIGH, x), high)
            low = jnp.where(at_y, spread_row(Y_LOW, x), none)
            low = jnp.where(at_x, spread_row(X_LOW, x), low)
            gain = jnp.where(upper, row(G_HIGH, x), row(G_LOW, x)).astype(BF16)
            both = jnp.concatenate([high, low, gain], axis=0)
            return total + lax.dot_general(both, own, NT, preferred_element_type=F32)

        acc[...] += lax.fori_loop(
            0, D_BLOCK, one_row, jnp.zeros(acc.shape, F32), unroll=D_BLOCK
        )
        return carry

    blocks = rows // D_BLOCK
    early = blocks // 2
    lax.fori_loop(0, early, pairs, 0)
    pl.semaphore_wait(barrier, n_member + 1)
    edges = [
        remote(s, d, edge_ssem.at[i], edge_rsem.at[i], t)
        for i, (s, d, t) in enumerate((
            (face_ref.at[0, pl.ds(rows - 8, 8), :], low_row_ref, (g_up, mi)),
            (face_ref.at[1, :, pl.ds(width - LANES, LANES)], below_w_ref, (gi, m_up)),
            (agg_ref.at[:, pl.ds(width - LANES, LANES)], below_a_ref, (gi, m_up)),
            (agg_ref.at[:, pl.ds(0, LANES)], above_a_ref, (gi, m_down)),
        ))
    ]
    for copy in edges:
        copy.start()


    def pack(t, carry):
        for i in range(STEP):
            fetch(t * STEP + i).wait()
        for i in range(STEP):
            x = t * STEP + i
            value = rhs[x]
            left = pltpu.roll(value[:, :LANES], x, 1)
            right = pltpu.roll(value[:, width - LANES:], lax.rem(rows + 1 + x, LANES), 1)
            carry = tuple(
                (jnp.where(lane == x + j, left, a), jnp.where(lane == rows + x - j, right, c))
                for j, (a, c) in enumerate(carry)
            )
        return carry

    blank = jnp.zeros((n_rhs, LANES), F32)
    packed = lax.fori_loop(0, rows // STEP, pack, ((blank, blank),) * DEPTH)
    packed = [
        jnp.where(lane < rows, turn(a, -j), turn(c, j)) for j, (a, c) in enumerate(packed)
    ]
    lax.fori_loop(early, blocks, pairs, 0)
    finish(edges)

    low_row = jnp.where(gi > 0, low_row_ref[7:8, :], 0.0)
    below = jnp.where(mi > 0, below_w_ref[:, LANES - 1:], 0.0)
    wx_low = wx_low + jnp.where(xs == 0, low_row, 0.0)
    wy_low = wy_low + jnp.where(ys == 0, below, 0.0)
    diagf = diag_ref[...] + wx + wy + wx_low + wy_low
    q = OMEGA / diagf
    last_x = (xs == rows - 1) & (gi == n_group - 1)
    last_y = (ys == width - 1) & (mi == n_member - 1)
    co[AX] = jnp.where(last_x, 0.0, q * wx)
    co[AX_LOW] = q * wx_low
    co[AY] = jnp.where(last_y, 0.0, q * wy)
    co[AY_LOW] = q * wy_low
    cf[Q - SIDES] = q
    cf[Q_INV - SIDES] = diagf * (1.0 / OMEGA)

    def scale(x, carry):
        b[x + 1] = rhs[x] * row(Q, x)
        return carry

    scale(0, 0)
    scale(rows - 1, 0)
    q_side = flip(q)
    b_cols = [pick(q_side, q_side, j) * packed[j] for j in range(DEPTH)]
    first = exchange(0, b, b_cols[0])
    interior(scale)

    def dot_high(left, right):
        return jnp.dot(
            left, right, precision=lax.Precision.HIGHEST, preferred_element_type=F32
        )

    lab = lax.broadcasted_iota(jnp.int32, (rows, LANES), 1)

    def hot_column(column):
        return jnp.where(column == lab, 1.0, 0.0)

    first_hot = hot_column(agg_ref[:, 0:1])
    last_hot = hot_column(agg_ref[:, width - 1:])
    above = jnp.where(mi < n_member - 1, face_ref[1, :, width - 1:], 0.0)
    first_sum = jnp.sum(first_hot * below, axis=0, keepdims=True)
    last_sum = jnp.sum(last_hot * above, axis=0, keepdims=True)
    low_sum = jnp.sum(hot[0].astype(F32) * low_row, axis=1, keepdims=True)
    eye = lax.broadcasted_iota(jnp.int32, (AGG, AGG), 0)
    eye = eye == lax.broadcasted_iota(jnp.int32, (AGG, AGG), 1)
    gain = acc[2 * AGG:2 * AGG + 1] + acc[2 * AGG + 8:2 * AGG + 9]
    half = jnp.where(eye, 0.5 * (low_sum + gain + first_sum), 0.0)
    half = half - acc[:AGG] - acc[AGG:2 * AGG]
    d_block = half + half.T
    table = jnp.zeros((rows, LANES), F32)
    for i, column in enumerate((
        agg_ref[:, 0:1], below_a_ref[:, LANES - 1:], below,
        agg_ref[:, width - 1:], above_a_ref[:, 0:1], above,
    )):
        table = jnp.where(lab == i, column.astype(F32), table)
    at_row = lax.broadcasted_iota(jnp.int32, (HALF, AGG), 0)
    at_lane = lax.broadcasted_iota(jnp.int32, (HALF, AGG), 1)
    upper_d, lower_d = d_block[:HALF], d_block[HALF:]
    folded = (at_lane >= HALF) & (at_lane - HALF <= at_row)
    mat[MAT_REACH, :HALF] = jnp.where(folded, pltpu.roll(upper_d, HALF, 1), lower_d)
    mat[MAT_REACH, HALF:, :rows] = table.T[:8]
    mat[MAT_REACH, HALF + 6:HALF + 7] = jnp.sum(
        jnp.where(at_lane - HALF == at_row, lower_d, 0.0), axis=0, keepdims=True
    )
    lm = jnp.sum(jnp.abs(d_block), axis=0, keepdims=True) + first_sum + last_sum
    lm_send[...] = jnp.broadcast_to(lm, lm_send.shape)
    lm_copies = []
    for off in range(1, n_member):
        peer = lax.rem(mi + off, n_member)
        copy = remote(
            lm_send, lm_recv.at[off - 1], lm_ssem.at[off - 1], lm_rsem.at[off - 1], (gi, peer)
        )
        copy.start()
        lm_copies.append(copy)
    ax_side, ax_low_side = flip(co[AX]), flip(co[AX_LOW])
    ay_side, ay_low_side = flip(co[AY]), flip(co[AY_LOW])
    agg_side = flip(cf[LABEL - SIDES])

    def column(buf, tile, cols, j):
        up, down = along_x(buf, cols[j], j)
        total = pick(ax_side, ax_side, j) * up + pick(ax_low_side, ax_low_side, j) * down
        outer = cols[j - 1] if j else tile
        total = total + pick(ay_side, ay_low_side, j) * cols[j + 1]
        return total + pick(ay_low_side, ay_side, j) * outer

    tile = halo(0, first)

    def pre(x, carry):
        cur, total = neighbours(b, co, x, tile)
        f[x + 1] = (2.0 - OMEGA) * cur + total
        return carry

    pre(0, 0)
    pre(rows - 1, 0)
    f_cols = [
        (2.0 - OMEGA) * b_cols[j] + column(b, tile, b_cols, j) for j in range(DEPTH - 1)
    ]
    second = exchange(1, f, f_cols[0])
    mats = spread_to(mat, mat_ssem, mat_rsem)
    interior(pre)

    def restrict(x, carry):
        cur, total = neighbours(f, co, x, None)
        resid = (b[x + 1] - OMEGA * cur + total) * row(Q_INV, x)
        high, low = split(resid)
        both = jnp.concatenate([high, low], axis=0)
        return carry + lax.dot_general(both, hot[x], NT, preferred_element_type=F32)

    tile = halo(1, second)
    sums = lax.fori_loop(
        0, rows, restrict, jnp.zeros((2 * n_rhs, AGG), F32), unroll=16
    )
    resid = sums[:n_rhs] + sums[n_rhs:]
    ends = jnp.concatenate([first_hot * below, last_hot * above], axis=0)
    resid = resid + dot_high(tile, ends)

    vec[VEC_REACH] = resid
    vecs = spread_to(vec, vec_ssem, vec_rsem)

    finish(lm_copies)
    lm8 = lm_send[...]
    for off in range(1, n_member):
        lm8 = jnp.maximum(lm8, lm_recv[off - 1])
    lmax = jnp.max(lm8[0:1], axis=1, keepdims=True)
    lmin = lmax / RATIO
    theta = (lmax + lmin) / 2.0
    delta = (lmax - lmin) / 2.0
    sigma = theta / delta
    rho = 1.0 / sigma
    collect(mats)
    place = lax.broadcasted_iota(jnp.int32, (AGG, LANES), 0).astype(F32)

    def couple(source, own, weight):
        value = jnp.where(place == own, weight, 0.0)
        both = jnp.concatenate(split(value), axis=0)
        hot_in = jnp.where(place == source, 1.0, 0.0).astype(BF16)
        prod = lax.dot_general(hot_in, both, NT, preferred_element_type=F32)
        return -(prod[:, :AGG] + prod[:, AGG:])

    for i in range(2 * MAT_REACH + 1):
        line = mat[i, HALF:]
        sent = mat[i, :HALF]
        turned = jnp.concatenate([sent, sent], axis=0).T
        lower_d = jnp.where(at_lane - HALF == at_row, line[6:7], turned[HALF:])
        lower_d = jnp.where((at_lane < HALF) | (at_lane - HALF > at_row), sent, lower_d)
        upper_d = jnp.where(at_lane <= at_row, pltpu.roll(sent, HALF, 1), turned[HALF:])
        upper_d = jnp.where(at_lane < HALF, upper_d, turned[:HALF])
        parts = (
            jnp.concatenate([upper_d, lower_d], axis=0),
            couple(line[1:2], line[0:1], line[2:3]),
            couple(line[4:5], line[3:4], line[5:6]),
        )
        for k, part in enumerate(parts):
            blocks_w[i, k * AGG:(k + 1) * AGG, :] = jnp.concatenate(split(part), axis=1)

    def product(at, dirs):
        column = jnp.concatenate([dirs[at], dirs[at - 1], dirs[at + 1]], axis=1)
        both = jnp.concatenate(split(column), axis=0)
        prod = jnp.dot(both, blocks_w[at + MAT_REACH], preferred_element_type=F32)
        prod = prod[:n_rhs] + prod[n_rhs:]
        return prod[:, :AGG] + prod[:, AGG:]

    collect(vecs)
    reach = VEC_REACH
    res = {at: vec[at + reach] for at in range(-reach, reach + 1)}
    dirs = {at: value / theta for at, value in res.items()}
    sol = jnp.zeros_like(resid)
    for step in range(CHEB):
        sol = sol + dirs[0]
        if step + 1 < CHEB:
            reach -= 1
            rho_new = 1.0 / (2.0 * sigma - rho)
            own_scale, res_scale = rho_new * rho, 2.0 * rho_new / delta
            inside = range(-reach, reach + 1)
            res = {at: res[at] - product(at, dirs) for at in inside}
            dirs = {at: own_scale * dirs[at] + res_scale * res[at] for at in inside}
            rho = rho_new

    e_high, e_low = split(sol)
    e_both = jnp.concatenate([e_high, e_low], axis=0)

    def prolong(x, carry):
        spread = jnp.dot(e_both, hot[x], preferred_element_type=F32)
        g[x + 1] = f[x + 1] + spread[:n_rhs] + spread[n_rhs:]
        return carry

    def prolong_column(j):
        hot_side = jnp.where(place == pick(agg_side, agg_side, j), 1.0, 0.0).astype(BF16)
        spread = jnp.dot(e_both, hot_side, preferred_element_type=F32)
        return f_cols[j] + spread[:n_rhs] + spread[n_rhs:]

    prolong(0, 0)
    prolong(rows - 1, 0)
    g_cols = [prolong_column(j) for j in range(DEPTH - 1)]
    third = exchange(2, g, g_cols[0])
    interior(prolong)
    tile = halo(2, third)

    def post(x, carry):
        cur, total = neighbours(g, co, x, tile)
        h[x + 1] = b[x + 1] + (1.0 - OMEGA) * cur + total
        return carry

    post(0, 0)
    post(rows - 1, 0)
    h_col = b_cols[0] + (1.0 - OMEGA) * g_cols[0] + column(g, tile, g_cols, 0)
    fourth = exchange(3, h, h_col)
    interior(post)
    side[...] = halo(3, fourth)
    for copy in started:
        copy.wait_send()
    for sends, copy in partial:
        pl.when(sends)(copy.wait_send)


def local(right_side, diagonal, face_weight, aggregation):
    n_group, n_member = lax.axis_size("group"), lax.axis_size("member")
    n_rhs, rows, width = right_side.shape
    n_vec, n_mat = 2 * VEC_REACH + 1, 2 * MAT_REACH + 1
    padded = pltpu.VMEM((rows + 2, n_rhs, width), F32)
    dma = pltpu.SemaphoreType.DMA
    vmem = pl.BlockSpec(memory_space=pltpu.VMEM)
    strip = pltpu.VMEM((rows, LANES), jnp.int32)
    h, b, co, side = pl.pallas_call(
        functools.partial(cycle_kernel, n_group, n_member),
        out_shape=[
            jax.ShapeDtypeStruct(shape, F32)
            for shape in (
                (rows + 2, n_rhs, width), (rows + 2, n_rhs, width), (SIDES, rows, width), (n_rhs, LANES)
            )
        ],
        in_specs=[pl.BlockSpec(memory_space=pl.ANY)] * 4,
        out_specs=[vmem] * 4,
        scratch_shapes=[
            pltpu.VMEM((rows, n_rhs, width), F32),
            pltpu.VMEM((PLANES - SIDES, rows, width), F32),
            pltpu.VMEM((rows, AGG, width), BF16),
            pltpu.VMEM((2 * AGG + 16, AGG), F32),
            pltpu.VMEM((rows, width), F32),
            pltpu.VMEM((2, rows, width), F32),
            pltpu.VMEM((rows, width), jnp.int32),
            pltpu.VMEM((8, width), F32),
            pltpu.VMEM((rows, LANES), F32),
            strip, strip,
            padded, padded,
            pltpu.VMEM((4, n_rhs, LANES), F32),
            pltpu.VMEM((4, 2, n_rhs, LANES), F32),
            pltpu.VMEM((n_vec, n_rhs, AGG), F32),
            pltpu.VMEM((8, AGG), F32),
            pltpu.VMEM((n_member - 1, 8, AGG), F32),
            pltpu.VMEM((n_mat, HALF + 8, AGG), F32),
            pltpu.VMEM((n_mat, 3 * AGG, 2 * AGG), BF16),
            dma((rows,)), dma((3,)), dma((4,)), dma((4,)), dma((4, 4)), dma((4, 4)),
            dma((n_vec,)), dma((n_vec,)), dma((n_mat,)), dma((n_mat,)),
            dma((n_member - 1,)), dma((n_member - 1,)),
        ],
        compiler_params=pltpu.CompilerParams(
            collective_id=0, has_side_effects=True, vmem_limit_bytes=40 * 1024 * 1024
        ),
    )(*(
        pltpu.with_memory_space_constraint(x, pltpu.HBM)
        for x in (right_side, diagonal, face_weight, aggregation)
    ))
    return pl.pallas_call(
        final_kernel,
        out_shape=jax.ShapeDtypeStruct(right_side.shape, F32),
        in_specs=[vmem] * 4,
        out_specs=pl.BlockSpec(memory_space=pl.ANY),
        scratch_shapes=[pltpu.VMEM((rows, n_rhs, width), F32), dma((rows,))],
        compiler_params=pltpu.CompilerParams(vmem_limit_bytes=16 * 1024 * 1024),
    )(h, b, co, side)


def solution(mesh):
    placed = (
        P(None, "group", "member"),
        P("group", "member"),
        P(None, "group", "member"),
        P("group", "member"),
    )
    return jax.shard_map(
        local, mesh=mesh, in_specs=placed, out_specs=P(None, "group", "member"), check_vma=False
    )
```

```python
import functools

import jax
import jax.numpy as jnp
from jax import lax
from jax.experimental import pallas as pl
from jax.experimental.pallas import tpu as pltpu
from jax.sharding import PartitionSpec as P

AGG = 128
POST = 2
CHEB = 6
OMEGA = 0.8
RATIO = 30.0
LANES = 128
MESH = pl.DeviceIdType.MESH
F32 = jnp.float32
BF16 = jnp.bfloat16
NT = (((1,), (1,)), ((), ()))


def split(value):
    high = value.astype(BF16)
    return high, (value - high.astype(F32)).astype(BF16)


AX, AX_LOW, AY, AY_LOW = range(4)
SIDES = 4
Q, Q_INV = 4, 5
LABEL, LABEL_X, LABEL_Y, X_HIGH, X_LOW, Y_HIGH, Y_LOW, G_HIGH, G_LOW = range(6, 15)
PLANES = 15
D_BLOCK = 16
HALF = AGG // 2
STEP = 16
DEPTH = 3
VEC_REACH = CHEB - 1
MAT_REACH = CHEB - 2


def lanes_of(n_rhs):
    return lax.broadcasted_iota(jnp.int32, (n_rhs, LANES), 1)


def neighbours(buf, co, x, tile):
    rows, n_rhs, width = buf.shape[0] - 2, buf.shape[1], buf.shape[2]
    tiles = width // LANES
    lane = lanes_of(n_rhs)
    cur = buf[x + 1]
    parts = [cur[:, k * LANES:(k + 1) * LANES] for k in range(tiles)]
    if tile is None:
        before = after = jnp.zeros((n_rhs, LANES), F32)
    else:
        before = pltpu.roll(tile, lax.rem(LANES - x, LANES), 1)
        after = pltpu.roll(tile, LANES - 1 - rows - x, 1)
    right = [before] + [pltpu.roll(p, 1, 1) for p in parts]
    left = [pltpu.roll(p, LANES - 1, 1) for p in parts] + [after]
    low = [jnp.where(lane == 0, right[k], right[k + 1]) for k in range(tiles)]
    high = [jnp.where(lane == LANES - 1, left[k + 1], left[k]) for k in range(tiles)]
    low = jnp.concatenate(low, axis=1)
    high = jnp.concatenate(high, axis=1)
    at = pl.ds(x, 1)
    total = co[AX, at, :] * buf[x + 2] + co[AX_LOW, at, :] * buf[x]
    return cur, total + co[AY, at, :] * high + co[AY_LOW, at, :] * low


def final_kernel(h, b, co, side, out_hbm, out, sem):
    rows = out.shape[0]
    tile = side[...]

    def copy(x):
        return pltpu.make_async_copy(out.at[x], out_hbm.at[:, x, :], sem.at[x])

    def step(t, carry):
        for i in range(STEP):
            x = t * STEP + i
            cur, total = neighbours(h, co, x, tile)
            out[x] = b[x + 1] + (1.0 - OMEGA) * cur + total
        for i in range(STEP):
            copy(t * STEP + i).start()
        return carry

    def wait(x, carry):
        copy(x).wait()
        return carry

    lax.fori_loop(0, rows // STEP, step, 0)
    lax.fori_loop(0, rows, wait, 0)


def cycle_kernel(
    n_group, n_member, rhs_hbm, diag_hbm, face_hbm, agg_hbm, h, b, co, side,
    rhs, cf, hot, acc, diag_ref, face_ref, agg_ref, low_row_ref, below_w_ref, below_a_ref, above_a_ref,
    f, g, col_send, col_recv, vec, lm_send, lm_recv, mat, blocks_w,
    rhs_sem, in_sem, edge_ssem, edge_rsem, halo_ssem, halo_rsem, vec_ssem, vec_rsem, mat_ssem, mat_rsem, lm_ssem, lm_rsem,
):
    rows, n_rhs, width = rhs.shape
    gi = lax.axis_index("group")
    mi = lax.axis_index("member")
    g_up, g_down = lax.rem(gi + 1, n_group), lax.rem(gi + n_group - 1, n_group)
    m_up, m_down = lax.rem(mi + 1, n_member), lax.rem(mi + n_member - 1, n_member)

    def is_member(off):
        return (mi + off >= 0) & (mi + off < n_member)

    def fetch(x):
        return pltpu.make_async_copy(rhs_hbm.at[:, x, :], rhs.at[x], rhs_sem.at[x])

    def start_fetch(x, carry):
        fetch(x).start()
        return carry

    loads = [
        pltpu.make_async_copy(src, dst, in_sem.at[i])
        for i, (src, dst) in enumerate((
            (face_hbm, face_ref), (diag_hbm, diag_ref), (agg_hbm, agg_ref)
        ))
    ]
    for load in loads:
        load.start()
    lax.fori_loop(0, rows, start_fetch, 0)

    vec[...] = jnp.zeros_like(vec)
    mat[...] = jnp.zeros_like(mat)
    col_recv[...] = jnp.zeros_like(col_recv)
    for buf in (b, f, g, h):
        buf[0] = jnp.zeros(buf.shape[1:], F32)
        buf[rows + 1] = jnp.zeros(buf.shape[1:], F32)
    barrier = pltpu.get_barrier_semaphore()
    for peer in (g_up, g_down):
        pl.semaphore_signal(barrier, inc=1, device_id=(peer, mi), device_id_type=MESH)
    for off in range(1, n_member):
        peer = lax.rem(mi + off, n_member)
        pl.semaphore_signal(barrier, inc=1, device_id=(gi, peer), device_id_type=MESH)

    lane = lanes_of(n_rhs)
    label = lax.broadcasted_iota(jnp.int32, (AGG, width), 0).astype(F32).astype(BF16)
    one, none = jnp.ones((), BF16), jnp.zeros((), BF16)

    def interior(body):
        whole = (rows - 2) // STEP * STEP
        lax.fori_loop(1, 1 + whole, body, 0, unroll=STEP)
        if whole < rows - 2:
            lax.fori_loop(1 + whole, rows - 1, body, 0, unroll=rows - 2 - whole)

    def remote(src, dst, ssem, rsem, target):
        return pltpu.make_async_remote_copy(
            src_ref=src, dst_ref=dst, send_sem=ssem, recv_sem=rsem,
            device_id=target, device_id_type=MESH,
        )

    can_up, can_down = gi < n_group - 1, gi > 0

    def exchange(phase, buf, tile):
        col_send[phase] = tile
        plan = (
            (buf.at[rows], buf.at[0], (g_up, mi), can_up, can_down),
            (buf.at[1], buf.at[rows + 1], (g_down, mi), can_down, can_up),
            (col_send.at[phase], col_recv.at[phase, 0], (gi, m_up), is_member(1), is_member(-1)),
            (col_send.at[phase], col_recv.at[phase, 1], (gi, m_down), is_member(-1), is_member(1)),
        )
        copies = []
        for i, (src, dst, target, sends, gets) in enumerate(plan):
            copy = remote(src, dst, halo_ssem.at[phase, i], halo_rsem.at[phase, i], target)
            pl.when(sends)(copy.start)
            copies.append((sends, gets, copy))
        return copies

    def halo(phase, copies):
        for _, gets, copy in copies:
            pl.when(gets)(copy.wait_recv)
        partial.extend((sends, copy) for sends, _, copy in copies)
        both = jnp.where(lane >= rows, col_recv[phase, 0], col_recv[phase, 1])
        return pltpu.roll(both, rows, 1)

    started = []

    def finish(copies):
        for copy in copies:
            copy.wait_recv()
        started.extend(copies)

    def spread_to(buf, ssem, rsem):
        reach = buf.shape[0] // 2
        copies = []
        for off in sorted(range(-reach, reach + 1), key=lambda o: -abs(o)):
            if off != 0:
                target = lax.rem(mi + off + 2 * n_member, n_member)
                copies.append((off, remote(
                    buf.at[reach], buf.at[reach - off], ssem.at[reach + off], rsem.at[reach - off], (gi, target)
                )))
        for off, copy in copies:
            pl.when(is_member(off))(copy.start)
        return copies

    partial = []

    def collect(copies):
        for off, copy in copies:
            pl.when(is_member(-off))(copy.wait_recv)
        partial.extend((is_member(off), copy) for off, copy in copies)

    def turn(value, shift):
        return pltpu.roll(value, shift % LANES, 1) if shift % LANES else value

    def along_x(buf, tile, j):
        first, last = buf[0], buf[rows + 1]
        down, up = turn(tile, 1), turn(tile, -1)
        down = jnp.where(lane == 0, turn(first[:, :LANES], -j), down)
        down = jnp.where(lane == rows, turn(first[:, width - LANES:], rows + 1 + j), down)
        up = jnp.where(lane == rows - 1, turn(last[:, :LANES], rows - 1 - j), up)
        up = jnp.where(lane == LANES - 1, turn(last[:, width - LANES:], j), up)
        return up, down

    def flip(plane):
        return jnp.concatenate([plane[:, :LANES], plane[:, width - LANES:]], axis=0).T

    at_left = lax.broadcasted_iota(jnp.int32, (1, LANES), 1) < rows

    def pick(left, right, j):
        return jnp.where(at_left, left[j:j + 1], right[LANES - 1 - j:LANES - j])

    def row(plane, x):
        return cf[plane - SIDES, pl.ds(x, 1), :]

    def narrow(plane, x):
        return jnp.broadcast_to(row(plane, x), (16, width)).astype(BF16)

    def spread_row(plane, x):
        return jnp.concatenate([narrow(plane, x)] * (AGG // 16), axis=0)

    for load in loads:
        load.wait()
    wx, wy, agg = face_ref[0], face_ref[1], agg_ref[...].astype(F32)
    xs = lax.broadcasted_iota(jnp.int32, (rows, width), 0)
    ys = lax.broadcasted_iota(jnp.int32, (rows, width), 1)
    wx_low = jnp.where(xs == 0, 0.0, pltpu.roll(wx, 1, 0))
    wy_low = jnp.where(ys == 0, 0.0, pltpu.roll(wy, 1, 1))
    own_diag = diag_ref[...] + wx + wy + wx_low + wy_low
    cf[LABEL - SIDES] = agg
    cf[LABEL_X - SIDES] = pltpu.roll(agg, rows - 1, 0)
    cf[LABEL_Y - SIDES] = pltpu.roll(agg, width - 1, 1)
    inner_y = jnp.where(ys == width - 1, 0.0, wy)
    inner_x = jnp.where(xs == rows - 1, 0.0, wx)
    inner_x = inner_x + jnp.where(cf[LABEL_X - SIDES] == cf[LABEL_Y - SIDES], inner_y, 0.0)
    for plane, value in ((X_HIGH, inner_x), (Y_HIGH, inner_y), (G_HIGH, own_diag)):
        high = value.astype(BF16).astype(F32)
        cf[plane - SIDES] = high
        cf[plane + 1 - SIDES] = value - high
    acc[...] = jnp.zeros_like(acc)

    upper = lax.broadcasted_iota(jnp.int32, (16, width), 0) < 8

    def pairs(block, carry):
        def one_row(i, total):
            x = block * D_BLOCK + i
            own = jnp.where(label == spread_row(LABEL, x), one, none)
            hot[x] = own
            at_x = label == spread_row(LABEL_X, x)
            at_y = label == spread_row(LABEL_Y, x)
            high = jnp.where(at_y, spread_row(Y_HIGH, x), none)
            high = jnp.where(at_x, spread_row(X_HIGH, x), high)
            low = jnp.where(at_y, spread_row(Y_LOW, x), none)
            low = jnp.where(at_x, spread_row(X_LOW, x), low)
            gain = jnp.where(upper, row(G_HIGH, x), row(G_LOW, x)).astype(BF16)
            both = jnp.concatenate([high, low, gain], axis=0)
            return total + lax.dot_general(both, own, NT, preferred_element_type=F32)

        acc[...] += lax.fori_loop(
            0, D_BLOCK, one_row, jnp.zeros(acc.shape, F32), unroll=D_BLOCK
        )
        return carry

    blocks = rows // D_BLOCK
    early = 1
    lax.fori_loop(0, early, pairs, 0)
    pl.semaphore_wait(barrier, n_member + 1)
    edges = [
        remote(s, d, edge_ssem.at[i], edge_rsem.at[i], t)
        for i, (s, d, t) in enumerate((
            (face_ref.at[0, pl.ds(rows - 8, 8), :], low_row_ref, (g_up, mi)),
            (face_ref.at[1, :, pl.ds(width - LANES, LANES)], below_w_ref, (gi, m_up)),
            (agg_ref.at[:, pl.ds(width - LANES, LANES)], below_a_ref, (gi, m_up)),
            (agg_ref.at[:, pl.ds(0, LANES)], above_a_ref, (gi, m_down)),
        ))
    ]
    for copy in edges:
        copy.start()


    def pack(t, carry):
        for i in range(STEP):
            fetch(t * STEP + i).wait()
        for i in range(STEP):
            x = t * STEP + i
            value = rhs[x]
            left = pltpu.roll(value[:, :LANES], x, 1)
            right = pltpu.roll(value[:, width - LANES:], lax.rem(rows + 1 + x, LANES), 1)
            carry = tuple(
                (jnp.where(lane == x + j, left, a), jnp.where(lane == rows + x - j, right, c))
                for j, (a, c) in enumerate(carry)
            )
        return carry

    blank = jnp.zeros((n_rhs, LANES), F32)
    packed = lax.fori_loop(0, rows // STEP, pack, ((blank, blank),) * DEPTH)
    packed = [
        jnp.where(lane < rows, turn(a, -j), turn(c, j)) for j, (a, c) in enumerate(packed)
    ]
    lax.fori_loop(early, blocks - 1, pairs, 0)
    finish(edges)

    low_row = jnp.where(gi > 0, low_row_ref[7:8, :], 0.0)
    below = jnp.where(mi > 0, below_w_ref[:, LANES - 1:], 0.0)
    wx_low = wx_low + jnp.where(xs == 0, low_row, 0.0)
    wy_low = wy_low + jnp.where(ys == 0, below, 0.0)
    diagf = diag_ref[...] + wx + wy + wx_low + wy_low
    q = OMEGA / diagf
    last_x = (xs == rows - 1) & (gi == n_group - 1)
    last_y = (ys == width - 1) & (mi == n_member - 1)
    co[AX] = jnp.where(last_x, 0.0, q * wx)
    co[AX_LOW] = q * wx_low
    co[AY] = jnp.where(last_y, 0.0, q * wy)
    co[AY_LOW] = q * wy_low
    cf[Q - SIDES] = q
    cf[Q_INV - SIDES] = diagf * (1.0 / OMEGA)

    def scale(x, carry):
        b[x + 1] = rhs[x] * row(Q, x)
        return carry

    scale(0, 0)
    scale(rows - 1, 0)
    q_side = flip(q)
    b_cols = [pick(q_side, q_side, j) * packed[j] for j in range(DEPTH)]
    first = exchange(0, b, b_cols[0])
    interior(scale)
    lax.fori_loop(blocks - 1, blocks, pairs, 0)

    def dot_high(left, right):
        return jnp.dot(
            left, right, precision=lax.Precision.HIGHEST, preferred_element_type=F32
        )

    lab = lax.broadcasted_iota(jnp.int32, (rows, LANES), 1)

    def hot_column(column):
        return jnp.where(column == lab, 1.0, 0.0)

    first_hot = hot_column(agg_ref[:, 0:1])
    last_hot = hot_column(agg_ref[:, width - 1:])
    above = jnp.where(mi < n_member - 1, face_ref[1, :, width - 1:], 0.0)
    first_sum = jnp.sum(first_hot * below, axis=0, keepdims=True)
    last_sum = jnp.sum(last_hot * above, axis=0, keepdims=True)
    low_sum = jnp.sum(hot[0].astype(F32) * low_row, axis=1, keepdims=True)
    eye = lax.broadcasted_iota(jnp.int32, (AGG, AGG), 0)
    eye = eye == lax.broadcasted_iota(jnp.int32, (AGG, AGG), 1)
    gain = acc[2 * AGG:2 * AGG + 1] + acc[2 * AGG + 8:2 * AGG + 9]
    half = jnp.where(eye, 0.5 * (low_sum + gain + first_sum), 0.0)
    half = half - acc[:AGG] - acc[AGG:2 * AGG]
    d_block = half + half.T
    table = jnp.zeros((rows, LANES), F32)
    for i, column in enumerate((
        agg_ref[:, 0:1], below_a_ref[:, LANES - 1:], below,
        agg_ref[:, width - 1:], above_a_ref[:, 0:1], above,
    )):
        table = jnp.where(lab == i, column.astype(F32), table)
    at_row = lax.broadcasted_iota(jnp.int32, (HALF, AGG), 0)
    at_lane = lax.broadcasted_iota(jnp.int32, (HALF, AGG), 1)
    upper_d, lower_d = d_block[:HALF], d_block[HALF:]
    folded = (at_lane >= HALF) & (at_lane - HALF <= at_row)
    mat[MAT_REACH, :HALF] = jnp.where(folded, pltpu.roll(upper_d, HALF, 1), lower_d)
    mat[MAT_REACH, HALF:, :rows] = table.T[:8]
    mat[MAT_REACH, HALF + 6:HALF + 7] = jnp.sum(
        jnp.where(at_lane - HALF == at_row, lower_d, 0.0), axis=0, keepdims=True
    )
    lm = jnp.sum(jnp.abs(d_block), axis=0, keepdims=True) + first_sum + last_sum
    lm_send[...] = jnp.broadcast_to(lm, lm_send.shape)
    lm_copies = []
    for off in range(1, n_member):
        peer = lax.rem(mi + off, n_member)
        copy = remote(
            lm_send, lm_recv.at[off - 1], lm_ssem.at[off - 1], lm_rsem.at[off - 1], (gi, peer)
        )
        copy.start()
        lm_copies.append(copy)
    ax_side, ax_low_side = flip(co[AX]), flip(co[AX_LOW])
    ay_side, ay_low_side = flip(co[AY]), flip(co[AY_LOW])
    agg_side = flip(cf[LABEL - SIDES])

    def column(buf, tile, cols, j):
        up, down = along_x(buf, cols[j], j)
        total = pick(ax_side, ax_side, j) * up + pick(ax_low_side, ax_low_side, j) * down
        outer = cols[j - 1] if j else tile
        total = total + pick(ay_side, ay_low_side, j) * cols[j + 1]
        return total + pick(ay_low_side, ay_side, j) * outer

    tile = halo(0, first)

    def pre(x, carry):
        cur, total = neighbours(b, co, x, tile)
        f[x + 1] = (2.0 - OMEGA) * cur + total
        return carry

    pre(0, 0)
    pre(rows - 1, 0)
    f_cols = [
        (2.0 - OMEGA) * b_cols[j] + column(b, tile, b_cols, j) for j in range(DEPTH - 1)
    ]
    second = exchange(1, f, f_cols[0])
    mats = spread_to(mat, mat_ssem, mat_rsem)
    interior(pre)

    def restrict(x, carry):
        cur, total = neighbours(f, co, x, None)
        resid = (b[x + 1] - OMEGA * cur + total) * row(Q_INV, x)
        high, low = split(resid)
        both = jnp.concatenate([high, low], axis=0)
        return carry + lax.dot_general(both, hot[x], NT, preferred_element_type=F32)

    tile = halo(1, second)
    sums = lax.fori_loop(
        0, rows, restrict, jnp.zeros((2 * n_rhs, AGG), F32), unroll=16
    )
    resid = sums[:n_rhs] + sums[n_rhs:]
    ends = jnp.concatenate([first_hot * below, last_hot * above], axis=0)
    resid = resid + dot_high(tile, ends)

    vec[VEC_REACH] = resid
    vecs = spread_to(vec, vec_ssem, vec_rsem)

    finish(lm_copies)
    lm8 = lm_send[...]
    for off in range(1, n_member):
        lm8 = jnp.maximum(lm8, lm_recv[off - 1])
    lmax = jnp.max(lm8[0:1], axis=1, keepdims=True)
    lmin = lmax / RATIO
    theta = (lmax + lmin) / 2.0
    delta = (lmax - lmin) / 2.0
    sigma = theta / delta
    rho = 1.0 / sigma
    collect(mats)
    place = lax.broadcasted_iota(jnp.int32, (AGG, LANES), 0).astype(F32)

    def couple(source, own, weight):
        value = jnp.where(place == own, weight, 0.0)
        both = jnp.concatenate(split(value), axis=0)
        hot_in = jnp.where(place == source, 1.0, 0.0).astype(BF16)
        prod = lax.dot_general(hot_in, both, NT, preferred_element_type=F32)
        return -(prod[:, :AGG] + prod[:, AGG:])

    for i in range(2 * MAT_REACH + 1):
        line = mat[i, HALF:]
        sent = mat[i, :HALF]
        turned = jnp.concatenate([sent, sent], axis=0).T
        lower_d = jnp.where(at_lane - HALF == at_row, line[6:7], turned[HALF:])
        lower_d = jnp.where((at_lane < HALF) | (at_lane - HALF > at_row), sent, lower_d)
        upper_d = jnp.where(at_lane <= at_row, pltpu.roll(sent, HALF, 1), turned[HALF:])
        upper_d = jnp.where(at_lane < HALF, upper_d, turned[:HALF])
        parts = (
            jnp.concatenate([upper_d, lower_d], axis=0),
            couple(line[1:2], line[0:1], line[2:3]),
            couple(line[4:5], line[3:4], line[5:6]),
        )
        for k, part in enumerate(parts):
            blocks_w[i, k * AGG:(k + 1) * AGG, :] = jnp.concatenate(split(part), axis=1)

    def product(at, dirs):
        column = jnp.concatenate([dirs[at], dirs[at - 1], dirs[at + 1]], axis=1)
        both = jnp.concatenate(split(column), axis=0)
        prod = jnp.dot(both, blocks_w[at + MAT_REACH], preferred_element_type=F32)
        prod = prod[:n_rhs] + prod[n_rhs:]
        return prod[:, :AGG] + prod[:, AGG:]

    collect(vecs)
    reach = VEC_REACH
    res = {at: vec[at + reach] for at in range(-reach, reach + 1)}
    dirs = {at: value / theta for at, value in res.items()}
    sol = jnp.zeros_like(resid)
    for step in range(CHEB):
        sol = sol + dirs[0]
        if step + 1 < CHEB:
            reach -= 1
            rho_new = 1.0 / (2.0 * sigma - rho)
            own_scale, res_scale = rho_new * rho, 2.0 * rho_new / delta
            inside = range(-reach, reach + 1)
            res = {at: res[at] - product(at, dirs) for at in inside}
            dirs = {at: own_scale * dirs[at] + res_scale * res[at] for at in inside}
            rho = rho_new

    e_high, e_low = split(sol)
    e_both = jnp.concatenate([e_high, e_low], axis=0)

    def prolong(x, carry):
        spread = jnp.dot(e_both, hot[x], preferred_element_type=F32)
        g[x + 1] = f[x + 1] + spread[:n_rhs] + spread[n_rhs:]
        return carry

    def prolong_column(j):
        hot_side = jnp.where(place == pick(agg_side, agg_side, j), 1.0, 0.0).astype(BF16)
        spread = jnp.dot(e_both, hot_side, preferred_element_type=F32)
        return f_cols[j] + spread[:n_rhs] + spread[n_rhs:]

    prolong(0, 0)
    prolong(rows - 1, 0)
    g_cols = [prolong_column(j) for j in range(DEPTH - 1)]
    third = exchange(2, g, g_cols[0])
    interior(prolong)
    tile = halo(2, third)

    def post(x, carry):
        cur, total = neighbours(g, co, x, tile)
        h[x + 1] = b[x + 1] + (1.0 - OMEGA) * cur + total
        return carry

    post(0, 0)
    post(rows - 1, 0)
    h_col = b_cols[0] + (1.0 - OMEGA) * g_cols[0] + column(g, tile, g_cols, 0)
    fourth = exchange(3, h, h_col)
    interior(post)
    side[...] = halo(3, fourth)
    for copy in started:
        copy.wait_send()
    for sends, copy in partial:
        pl.when(sends)(copy.wait_send)


def local(right_side, diagonal, face_weight, aggregation):
    n_group, n_member = lax.axis_size("group"), lax.axis_size("member")
    n_rhs, rows, width = right_side.shape
    n_vec, n_mat = 2 * VEC_REACH + 1, 2 * MAT_REACH + 1
    padded = pltpu.VMEM((rows + 2, n_rhs, width), F32)
    dma = pltpu.SemaphoreType.DMA
    vmem = pl.BlockSpec(memory_space=pltpu.VMEM)
    strip = pltpu.VMEM((rows, LANES), jnp.int32)
    h, b, co, side = pl.pallas_call(
        functools.partial(cycle_kernel, n_group, n_member),
        out_shape=[
            jax.ShapeDtypeStruct(shape, F32)
            for shape in (
                (rows + 2, n_rhs, width), (rows + 2, n_rhs, width), (SIDES, rows, width), (n_rhs, LANES)
            )
        ],
        in_specs=[pl.BlockSpec(memory_space=pl.ANY)] * 4,
        out_specs=[vmem] * 4,
        scratch_shapes=[
            pltpu.VMEM((rows, n_rhs, width), F32),
            pltpu.VMEM((PLANES - SIDES, rows, width), F32),
            pltpu.VMEM((rows, AGG, width), BF16),
            pltpu.VMEM((2 * AGG + 16, AGG), F32),
            pltpu.VMEM((rows, width), F32),
            pltpu.VMEM((2, rows, width), F32),
            pltpu.VMEM((rows, width), jnp.int32),
            pltpu.VMEM((8, width), F32),
            pltpu.VMEM((rows, LANES), F32),
            strip, strip,
            padded, padded,
            pltpu.VMEM((4, n_rhs, LANES), F32),
            pltpu.VMEM((4, 2, n_rhs, LANES), F32),
            pltpu.VMEM((n_vec, n_rhs, AGG), F32),
            pltpu.VMEM((8, AGG), F32),
            pltpu.VMEM((n_member - 1, 8, AGG), F32),
            pltpu.VMEM((n_mat, HALF + 8, AGG), F32),
            pltpu.VMEM((n_mat, 3 * AGG, 2 * AGG), BF16),
            dma((rows,)), dma((3,)), dma((4,)), dma((4,)), dma((4, 4)), dma((4, 4)),
            dma((n_vec,)), dma((n_vec,)), dma((n_mat,)), dma((n_mat,)),
            dma((n_member - 1,)), dma((n_member - 1,)),
        ],
        compiler_params=pltpu.CompilerParams(
            collective_id=0, has_side_effects=True, vmem_limit_bytes=40 * 1024 * 1024
        ),
    )(*(
        pltpu.with_memory_space_constraint(x, pltpu.HBM)
        for x in (right_side, diagonal, face_weight, aggregation)
    ))
    return pl.pallas_call(
        final_kernel,
        out_shape=jax.ShapeDtypeStruct(right_side.shape, F32),
        in_specs=[vmem] * 4,
        out_specs=pl.BlockSpec(memory_space=pl.ANY),
        scratch_shapes=[pltpu.VMEM((rows, n_rhs, width), F32), dma((rows,))],
        compiler_params=pltpu.CompilerParams(vmem_limit_bytes=16 * 1024 * 1024),
    )(h, b, co, side)


def solution(mesh):
    placed = (
        P(None, "group", "member"),
        P("group", "member"),
        P(None, "group", "member"),
        P("group", "member"),
    )
    return jax.shard_map(
        local, mesh=mesh, in_specs=placed, out_specs=P(None, "group", "member"), check_vma=False
    )
```
